128 devices in a mesh: seq: 64 (over z, y, x), ch: 2 (over core).
Axes of the slice: x: 4, y: 4, z: 4, core: 2. Of those that a mesh axis runs over, the one named last changes fastest.
Arguments:
- tokens: bfloat16 [32768, 2048], P('seq', 'ch'), may hold values from -6 to 6
- in_weight: bfloat16 [2048, 3, 2048], P(None, None, 'ch'), may hold values from -0.125 to 0.125
- short_filter: float32 [3, 3, 2048], P(None, None, 'ch'), may hold values from -3 to 3
- residues: float32 [2048, 16], P('ch'), may hold values from -3 to 3
- rates: float32 [2048, 16], P('ch'), as said below
- out_weight: bfloat16 [2048, 2048], P('ch'), may hold values from -0.1875 to 0.1875
Outputs:
- output: float32 [32768, 2048], P('seq', 'ch')
The draws below stay inside these ranges and needn't reach their ends.
Inputs may be any that keep to these rules, and one draw needn't show every extreme that they name: `rates`: every rate lies between 0.2 / 32768 and 1 / 30.
All inputs are finite; a program needn't handle non-finite values.
Results may differ from the reference program's by a relative error of at most 0.004.
Values may be sent and summed in bfloat16 or wider, within the bound.
No kernel may reach another device: no remote copies, remote signals or barrier semaphores. Data moves between devices by JAX's collectives and lax.ppermute only.
A program may use at most 192 MiB of HBM per device.

```python
import math
import jax
import jax.numpy as jnp
from jax import lax

D = 2048
MODES = 16
TOK_DEV = 512
LENGTH = 32768


def draw_rates(key, part):
    mask_key, slow_key, fast_key = jax.random.split(key, 3)
    slow_share = 0.5
    low_log = math.log(0.2 / LENGTH)
    mid_log = math.log(2.0 / LENGTH)
    high_log = math.log(1.0 / 30.0)
    slow_rates = jnp.exp(jax.random.uniform(slow_key, (D, MODES), jnp.float32, low_log, mid_log))
    fast_rates = jnp.exp(jax.random.uniform(fast_key, (D, MODES), jnp.float32, mid_log, high_log))
    slow_pick = jax.random.uniform(mask_key, (D, MODES), jnp.float32) < slow_share
    return jnp.where(slow_pick, slow_rates, fast_rates)


def raised(array, key, source, target, parts, factor):
    owner, partner = [(jnp.arange(array.shape[position]) // (array.shape[position] // parts)).reshape([-1 if axis == position else 1 for axis in range(array.ndim)]) for position in (source, target)]
    chosen = jax.random.permutation(key, parts)[partner]
    strong = (owner == chosen) | (owner == (partner + parts // 2) % parts)
    return jnp.where(strong, factor * array, array)


def level_of(rng, shape, shards, smallest, largest):
    def one(axis_at, parts):
        heights = jax.random.uniform(jax.random.fold_in(jax.random.fold_in(rng, 6), axis_at), (parts,), jnp.float32, smallest / len(shards), largest / len(shards))
        return jnp.repeat(jnp.exp(heights), shape[axis_at] // parts).reshape((-1,) + (1,) * (len(shape) - axis_at - 1))

    loudness = one(*shards[0])
    for cut in shards[1:]:
        loudness = loudness * one(*cut)
    return loudness


def gaussian(key, dims, width, limit, shards=(), held_as=jnp.bfloat16):
    entries = width * jax.random.normal(key, dims, jnp.float32)
    if shards:
        entries = entries * level_of(key, dims, shards, -0.22, 0.18)
    return jnp.clip(entries, -limit, limit).astype(held_as)


def gaussian_with(rng, shape, deviation, limit, pieces, heavy, kind=jnp.bfloat16):
    result = deviation * jax.random.normal(rng, shape, jnp.float32)
    if pieces:
        result = result * level_of(rng, shape, pieces, -0.22, 0.18)
    return jnp.clip(raised(result, jax.random.fold_in(rng, 3), *heavy), -limit, limit).astype(kind)


def setup_inputs(seed: int = 0) -> dict:
    seeds = jax.random.split(jax.random.key(seed), 7)
    return {
        "tokens": gaussian(seeds[0], (LENGTH, D), 1.0, 6.0, ((0, 64), (1, 2))),
        "in_weight": gaussian(seeds[1], (D, 3, D), D ** -0.5, 0.125, ((2, 2),)),
        "short_filter": gaussian(seeds[2], (3, 3, D), 0.6, 3.0, ((2, 2),), jnp.float32),
        "residues": gaussian(seeds[3], (D, MODES), 0.35, 3.0, ((0, 2),), jnp.float32),
        "rates": draw_rates(jax.random.fold_in(seeds[6], 71), 0),
        "out_weight": gaussian_with(seeds[5], (D, D), D ** -0.5, 0.1875, ((0, 2),), (0, 1, 2, 2.0)),
    }


def conv_tables(residues, rates, block_len):
    mode_gain = residues * jnp.sqrt(1.0 - jnp.exp(-2.0 * rates))
    lag_steps = jnp.arange(block_len, dtype=jnp.float32)[:, None, None]
    kernel = lax.optimization_barrier(jnp.sum(mode_gain * jnp.exp(-rates * lag_steps), axis=-1))
    offsets = jnp.arange(block_len)[:, None] - jnp.arange(block_len)[None, :]
    picked = jnp.take(kernel, jnp.maximum(offsets, 0), axis=0)
    toeplitz = jnp.where((offsets >= 0)[:, :, None], picked, jnp.zeros_like(picked))
    end_weights = jnp.exp(-rates * (block_len - 1.0 - lag_steps))
    lead_weights = mode_gain * jnp.exp(-rates * (lag_steps + 1.0))
    return (toeplitz, end_weights, lead_weights)

def block_terms(source, toeplitz, end_weights, block_len):
    blocks = source.reshape(-1, block_len, source.shape[1])
    local_part = jnp.einsum('tsg,bsg->btg', toeplitz, blocks, precision=lax.Precision.HIGHEST)
    block_ends = jnp.einsum('bsg,sgn->bgn', blocks, end_weights, precision=lax.Precision.HIGHEST)
    return (local_part, block_ends)

def carry_chain(block_ends, step_decay, start_state):

    def advance(carry_state, block_end):
        return (step_decay * carry_state + block_end, carry_state)
    last_state, states = lax.scan(advance, start_state, block_ends)
    return (states, last_state)

def apply_states(lead_weights, states):
    return jnp.einsum('tgn,bgn->btg', lead_weights, states, precision=lax.Precision.HIGHEST)

def reference(tokens, in_weight, short_filter, residues, rates, out_weight):
    length = tokens.shape[0]
    block_len = min(64, TOK_DEV)
    projected = jnp.dot(tokens, in_weight.reshape(D, 3 * D), preferred_element_type=jnp.float32).reshape(length, 3, D)
    padded = jnp.concatenate([jnp.zeros((2, 3, D), projected.dtype), projected], axis=0)
    filtered = short_filter[0] * padded[2:] + short_filter[1] * padded[1:-1] + short_filter[2] * padded[:-2]
    queries = filtered[:, 0, :]
    source = filtered[:, 1, :] * filtered[:, 2, :]
    group_width = math.gcd(D, 512)
    group_count = D // group_width

    def one_group(inputs):
        part_source, part_res, part_rates = inputs
        toeplitz, end_weights, lead_weights = conv_tables(part_res, part_rates, block_len)
        local_part, block_ends = block_terms(part_source, toeplitz, end_weights, block_len)
        step_decay = jnp.exp(-part_rates * block_len)
        states, last_state = carry_chain(block_ends, step_decay, jnp.zeros_like(part_rates))
        return (local_part + apply_states(lead_weights, states)).reshape(length, group_width)
    grouped = lax.map(one_group, (source.reshape(length, group_count, group_width).transpose(1, 0, 2), residues.reshape(group_count, group_width, MODES), rates.reshape(group_count, group_width, MODES)))
    convolved = grouped.transpose(1, 0, 2).reshape(length, D)
    hidden = (queries * convolved).astype(jnp.bfloat16)
    return jnp.dot(hidden, out_weight, preferred_element_type=jnp.float32)
```

```python
import jax
import jax.numpy as jnp
from jax import lax
from jax.experimental import pallas as pl
from jax.experimental.pallas import tpu as pltpu
from jax.sharding import Mesh, PartitionSpec as P

SEGS = 8
HALO = 16
LANES = 128
SEQ = ("z", "y", "x")
RING = 4
F32 = jnp.float32
BF16 = jnp.bfloat16
VMEM_LIMIT = 48 * 1024 * 1024


def spread(row):
    return jnp.broadcast_to(row, (SEGS, row.shape[-1]))


def filtered_step(taps, now, one, two):
    return taps[0] * now + taps[1] * one + taps[2] * two


def source_kernel(
    ch_ref,
    own_ref,
    other_ref,
    halo_own_ref,
    halo_other_ref,
    w_ref,
    filt_ref,
    rates_ref,
    lhs_ref,
    source_ref,
    ends_ref,
    total_ref,
    proj_ref,
    sems,
):
    rows = own_ref.shape[0]
    half = own_ref.shape[1]
    steps = rows // SEGS
    width = w_ref.shape[2]

    @pl.when(pl.program_id(0) == 0)
    def _():
        mine = pl.multiple_of(ch_ref[0] * half, half)
        theirs = pl.multiple_of((1 - ch_ref[0]) * half, half)
        copies = [
            pltpu.make_async_copy(
                src, lhs_ref.at[pl.ds(row, src.shape[0]), pl.ds(col, half)], sems.at[i]
            )
            for i, (src, row, col) in enumerate(
                (
                    (own_ref, HALO, mine),
                    (other_ref, HALO, theirs),
                    (halo_own_ref, 0, mine),
                    (halo_other_ref, 0, theirs),
                )
            )
        ]
        for copy in copies:
            copy.start()
        for copy in copies:
            copy.wait()

    lhs = lhs_ref[...]
    for j in range(2):
        part = jnp.dot(lhs, w_ref[j], preferred_element_type=F32)
        for i in range(width // LANES):
            proj_ref[j, i] = part[:, i * LANES : (i + 1) * LANES]

    for i in range(width // LANES):
        lanes = pl.ds(i * LANES, LANES)
        taps = [[spread(filt_ref[a, j + 1 : j + 2, lanes]) for a in range(3)] for j in range(2)]
        decays = [spread(jnp.exp(-rates_ref[n : n + 1, lanes])) for n in range(rates_ref.shape[0])]

        def at(j, t):
            return proj_ref[j, i, pl.ds(HALO + t, SEGS, stride=steps), :]

        def body(t, carry):
            k1, k2, v1, v2, states = carry
            k0, v0 = at(0, t), at(1, t)
            src = filtered_step(taps[0], k0, k1, k2) * filtered_step(taps[1], v0, v1, v2)
            source_ref[pl.ds(pl.multiple_of(t * SEGS, SEGS), SEGS), lanes] = src
            states = tuple(d * s + src for d, s in zip(decays, states))
            return k0, k1, v0, v1, states

        zero = jnp.zeros((SEGS, LANES), F32)
        carry = (at(0, -1), at(0, -2), at(1, -1), at(1, -2), (zero,) * len(decays))
        states = lax.fori_loop(0, steps, body, carry, unroll=8)[4]
        later = (SEGS - 1 - lax.broadcasted_iota(jnp.int32, (SEGS, LANES), 0)).astype(F32) * steps
        for n, state in enumerate(states):
            ends_ref[n * SEGS : (n + 1) * SEGS, lanes] = state
            weight = jnp.exp(-spread(rates_ref[n : n + 1, lanes]) * later)
            total_ref[n : n + 1, lanes] = jnp.sum(state * weight, axis=0, keepdims=True)


def source_call(ch, own, other, halo_own, halo_other, weight, filt, rates, width=256):
    rows, half = own.shape
    channels = weight.shape[2]
    modes = rates.shape[0]
    full = 2 * half
    grid_spec = pltpu.PrefetchScalarGridSpec(
        num_scalar_prefetch=1,
        grid=(channels // width,),
        in_specs=[pl.BlockSpec(memory_space=pl.ANY)] * 4
        + [
            pl.BlockSpec((pl.Element(2), pl.Element(full), pl.Element(width)), lambda i, c: (1, 0, i * width)),
            pl.BlockSpec((3, 3, width), lambda i, c: (0, 0, i)),
            pl.BlockSpec((modes, width), lambda i, c: (0, i)),
        ],
        out_specs=[
            pl.BlockSpec((HALO + rows, full), lambda i, c: (0, 0)),
            pl.BlockSpec((rows, width), lambda i, c: (0, i)),
            pl.BlockSpec((modes * SEGS, width), lambda i, c: (0, i)),
            pl.BlockSpec((modes, width), lambda i, c: (0, i)),
        ],
        scratch_shapes=[
            pltpu.VMEM((2, width // LANES, HALO + rows, LANES), F32),
            pltpu.SemaphoreType.DMA((4,)),
        ],
    )
    return pl.pallas_call(
        source_kernel,
        grid_spec=grid_spec,
        out_shape=[
            jax.ShapeDtypeStruct((HALO + rows, full), BF16),
            jax.ShapeDtypeStruct((rows, channels), F32),
            jax.ShapeDtypeStruct((modes * SEGS, channels), F32),
            jax.ShapeDtypeStruct((modes, channels), F32),
        ],
        compiler_params=pltpu.CompilerParams(vmem_limit_bytes=VMEM_LIMIT),
        name="source",
    )(ch, own, other, halo_own, halo_other, weight, filt, rates)


def query_kernel(lhs_ref, w_ref, filt_ref, query_ref, proj_ref):
    steps = query_ref.shape[0] // SEGS
    width = w_ref.shape[2]
    part = jnp.dot(lhs_ref[...], w_ref[0], preferred_element_type=F32)
    for i in range(width // LANES):
        proj_ref[i] = part[:, i * LANES : (i + 1) * LANES]
    for i in range(width // LANES):
        lanes = pl.ds(i * LANES, LANES)
        taps = [spread(filt_ref[a, 0:1, lanes]) for a in range(3)]

        def at(t):
            return proj_ref[i, pl.ds(HALO + t, SEGS, stride=steps), :]

        def body(t, carry):
            q1, q2 = carry
            q0 = at(t)
            query_ref[pl.ds(pl.multiple_of(t * SEGS, SEGS), SEGS), lanes] = filtered_step(
                taps, q0, q1, q2
            )
            return q0, q1

        lax.fori_loop(0, steps, body, (at(-1), at(-2)), unroll=8)


def query_call(lhs, weight, filt, width=256):
    rows = lhs.shape[0] - HALO
    full, channels = weight.shape[1:]
    return pl.pallas_call(
        query_kernel,
        grid=(channels // width,),
        in_specs=[
            pl.BlockSpec(lhs.shape, lambda i: (0, 0)),
            pl.BlockSpec((1, full, width), lambda i: (0, 0, i)),
            pl.BlockSpec((3, 3, width), lambda i: (0, 0, i)),
        ],
        out_specs=pl.BlockSpec((rows, width), lambda i: (0, i)),
        out_shape=jax.ShapeDtypeStruct((rows, channels), F32),
        scratch_shapes=[pltpu.VMEM((width // LANES, HALO + rows, LANES), F32)],
        compiler_params=pltpu.CompilerParams(vmem_limit_bytes=VMEM_LIMIT),
        name="query",
    )(lhs, weight, filt)


def local_kernel(source_ref, rates_ref, gain_ref, local_ref):
    steps = source_ref.shape[0] // SEGS
    modes = rates_ref.shape[0]
    decays = [spread(jnp.exp(-rates_ref[n : n + 1])) for n in range(modes)]
    gains = [spread(gain_ref[n : n + 1]) for n in range(modes)]

    def body(t, states):
        rows = pl.ds(pl.multiple_of(t * SEGS, SEGS), SEGS)
        src = source_ref[rows]
        states = tuple(d * s + src for d, s in zip(decays, states))
        parts = [g * s for g, s in zip(gains, states)]
        while len(parts) > 1:
            parts = [a + b for a, b in zip(parts[::2], parts[1::2])]
        local_ref[rows] = parts[0]
        return states

    zero = jnp.zeros((SEGS, LANES), F32)
    lax.fori_loop(0, steps, body, (zero,) * modes, unroll=8)


def local_call(source, rates, gain):
    rows, channels = source.shape
    modes = rates.shape[0]
    return pl.pallas_call(
        local_kernel,
        grid=(channels // LANES,),
        in_specs=[
            pl.BlockSpec((rows, LANES), lambda i: (0, i)),
            pl.BlockSpec((modes, LANES), lambda i: (0, i)),
            pl.BlockSpec((modes, LANES), lambda i: (0, i)),
        ],
        out_specs=pl.BlockSpec((rows, LANES), lambda i: (0, i)),
        out_shape=jax.ShapeDtypeStruct((rows, channels), F32),
        compiler_params=pltpu.CompilerParams(vmem_limit_bytes=VMEM_LIMIT),
        name="local",
    )(source, rates, gain)


def hidden_kernel(ends_ref, into_ref, local_ref, query_ref, rates_ref, gain_ref, hidden_ref):
    steps = local_ref.shape[0] // SEGS
    modes = rates_ref.shape[0]
    seg = lax.broadcasted_iota(jnp.int32, (SEGS, LANES), 0)
    decays, leads = [], []
    for n in range(modes):
        rate = spread(rates_ref[n : n + 1])
        state = pltpu.roll(ends_ref[n * SEGS : (n + 1) * SEGS], 1, 0)
        state = jnp.where(seg == 0, spread(into_ref[n : n + 1]), state)
        for hop in (1, 2, 4):
            earlier = pltpu.roll(state, hop, 0) * jnp.exp(-rate * float(steps * hop))
            state = state + jnp.where(seg >= hop, earlier, 0.0)
        decays.append(jnp.exp(-rate))
        leads.append(spread(gain_ref[n : n + 1]) * state)

    def body(t, leads):
        halves = []
        for u in range(2):
            rows = pl.ds(pl.multiple_of((2 * t + u) * SEGS, SEGS), SEGS)
            leads = tuple(d * s for d, s in zip(decays, leads))
            parts = list(leads)
            while len(parts) > 1:
                parts = [a + b for a, b in zip(parts[::2], parts[1::2])]
            halves.append(query_ref[rows] * (local_ref[rows] + parts[0]))
        rows = pl.ds(pl.multiple_of(2 * t * SEGS, 2 * SEGS), 2 * SEGS)
        hidden_ref[rows] = jnp.concatenate(halves, axis=0).astype(BF16)
        return leads

    lax.fori_loop(0, steps // 2, body, tuple(leads), unroll=4)


def hidden_call(ends, into, local, query, rates, gain):
    rows, channels = local.shape
    modes = rates.shape[0]

    def spec(count):
        return pl.BlockSpec((count, LANES), lambda i: (0, i))

    return pl.pallas_call(
        hidden_kernel,
        grid=(channels // LANES,),
        in_specs=[spec(modes * SEGS), spec(modes), spec(rows), spec(rows), spec(modes), spec(modes)],
        out_specs=spec(rows),
        out_shape=jax.ShapeDtypeStruct((rows, channels), BF16),
        compiler_params=pltpu.CompilerParams(vmem_limit_bytes=VMEM_LIMIT),
        name="hidden",
    )(ends, into, local, query, rates, gain)


def output_kernel(ch_ref, own_ref, other_ref, w_own_ref, w_other_ref, out_ref, acc_ref):
    rows, width = out_ref.shape
    steps = rows // SEGS
    part = jnp.dot(own_ref[...], w_own_ref[...], preferred_element_type=F32)
    part = part + jnp.dot(other_ref[...], w_other_ref[...], preferred_element_type=F32)
    for i in range(width // LANES):
        acc_ref[i] = part[:, i * LANES : (i + 1) * LANES]
    for i in range(width // LANES):
        for j in range(SEGS):
            out_ref[j * steps : (j + 1) * steps, i * LANES : (i + 1) * LANES] = acc_ref[
                i, pl.ds(j, steps, stride=SEGS), :
            ]


def output_call(ch, own, other, w_own, w_other, width=256):
    rows, channels = own.shape
    columns = w_own.shape[1] // 2
    tiles = columns // width
    grid_spec = pltpu.PrefetchScalarGridSpec(
        num_scalar_prefetch=1,
        grid=(tiles,),
        in_specs=[
            pl.BlockSpec((rows, channels), lambda i, c: (0, 0)),
            pl.BlockSpec((rows, channels), lambda i, c: (0, 0)),
            pl.BlockSpec((channels, width), lambda i, c: (0, c[0] * tiles + i)),
            pl.BlockSpec((channels, width), lambda i, c: (0, c[0] * tiles + i)),
        ],
        out_specs=pl.BlockSpec((rows, width), lambda i, c: (0, i)),
        scratch_shapes=[pltpu.VMEM((width // LANES, rows, LANES), F32)],
    )
    return pl.pallas_call(
        output_kernel,
        grid_spec=grid_spec,
        out_shape=jax.ShapeDtypeStruct((rows, columns), F32),
        compiler_params=pltpu.CompilerParams(vmem_limit_bytes=VMEM_LIMIT),
        name="output",
    )(ch, own, other, w_own, w_other)


def swapped(x):
    return lax.ppermute(x, "ch", [(0, 1), (1, 0)])


def from_before(x, crossed):
    count = RING**3
    pairs = [
        (2 * i + c, 2 * (i + 1) + (1 - c if crossed else c))
        for i in range(count - 1)
        for c in range(2)
    ]
    return lax.ppermute(x, (*SEQ, "ch"), pairs)


def ring_level(state, axis, rates, tokens):
    here = lax.axis_index(axis)
    sent = state.astype(BF16)
    arrived = [
        lax.ppermute(sent, axis, [(i, (i + k) % RING) for i in range(RING)]).astype(F32)
        for k in range(1, RING)
    ]
    before = jnp.zeros_like(state)
    total = state * jnp.exp(-rates * (tokens * (RING - 1 - here)).astype(F32))
    for k, part in zip(range(1, RING), arrived):
        weight = jnp.where(k <= here, jnp.exp(-rates * float(tokens * (k - 1))), 0.0)
        before = before + weight * part
        place = (here - k) % RING
        total = total + part * jnp.exp(-rates * (tokens * (RING - 1 - place)).astype(F32))
    return before, total


def on_device(tokens, in_weight, short_filter, residues, rates, out_weight):
    rows = tokens.shape[0]
    ch = lax.axis_index("ch").astype(jnp.int32).reshape(1)
    weight = in_weight.transpose(1, 0, 2)
    rates = rates.T
    gain = residues.T * jnp.sqrt(1.0 - jnp.exp(-2.0 * rates))

    other = swapped(tokens)
    last = tokens[rows - HALO :]
    halo_own = from_before(last, False)
    halo_other = from_before(last, True)
    out_weight_other = swapped(out_weight)

    lhs, source, ends, total = source_call(
        ch, tokens, other, halo_own, halo_other, weight, short_filter, rates
    )
    query = query_call(lhs, weight, short_filter)
    local = local_call(source, rates, gain)

    into = jnp.zeros_like(total)
    after = 0
    span = rows
    for axis in reversed(SEQ):
        before, total = ring_level(total, axis, rates, span)
        into = into + before * jnp.exp(-rates * jnp.asarray(after, F32))
        after = after + span * lax.axis_index(axis)
        span = span * RING

    hidden = hidden_call(ends, into, local, query, rates, gain)
    return output_call(ch, hidden, swapped(hidden), out_weight, out_weight_other)


def solution(mesh):
    cube = Mesh(mesh.devices.reshape(RING, RING, RING, 2), (*SEQ, "ch"))
    return jax.shard_map(
        on_device,
        mesh=cube,
        in_specs=(
            P(SEQ, "ch"),
            P(None, None, "ch"),
            P(None, None, "ch"),
            P("ch", None),
            P("ch", None),
            P("ch", None),
        ),
        out_specs=P(SEQ, "ch"),
        check_vma=False,
    )
```

```python
import jax
import jax.numpy as jnp
from jax import lax
from jax.experimental import pallas as pl
from jax.experimental.pallas import tpu as pltpu
from jax.sharding import Mesh, PartitionSpec as P

SEGS = 8
HALO = 16
LANES = 128
HISTORY = 8
WIDTH = 256
SEQ = ("z", "y", "x")
RING = 4
F32 = jnp.float32
BF16 = jnp.bfloat16
MIB = 1024 * 1024


def spread(row):
    return jnp.broadcast_to(row, (SEGS, row.shape[-1]))


def filtered_step(taps, now, one, two):
    return taps[0] * now + taps[1] * one + taps[2] * two


def tree_sum(parts):
    parts = list(parts)
    while len(parts) > 1:
        parts = [a + b for a, b in zip(parts[::2], parts[1::2])]
    return parts[0]


def stage_kernel(ch_ref, own_ref, other_ref, w_ref, filt_ref, rates_ref, lhs_out, w_out, filt_out, rates_out, sems):
    half = own_ref.shape[1]
    mine = pl.multiple_of(ch_ref[0] * half, half)
    theirs = pl.multiple_of((1 - ch_ref[0]) * half, half)
    pairs = [
        (own_ref, lhs_out.at[:, pl.ds(mine, half)]),
        (other_ref, lhs_out.at[:, pl.ds(theirs, half)]),
        (filt_ref, filt_out),
        (rates_ref, rates_out),
        (w_ref, w_out),
    ]
    copies = [pltpu.make_async_copy(src, dst, sems.at[i]) for i, (src, dst) in enumerate(pairs)]
    for copy in copies:
        copy.start()
    for copy in copies:
        copy.wait()


def stage_call(ch, own, other, weight, filt, rates):
    rows, half = own.shape
    vmem = pl.BlockSpec(memory_space=pltpu.VMEM)
    anywhere = pl.BlockSpec(memory_space=pl.ANY)
    inputs = [pltpu.with_memory_space_constraint(x, pltpu.HBM) for x in (own, weight, filt, rates)]
    return pl.pallas_call(
        stage_kernel,
        in_specs=[pl.BlockSpec(memory_space=pltpu.SMEM)] + [anywhere] * 5,
        out_specs=[vmem] * 4,
        out_shape=[
            pltpu.VMEM((rows, 2 * half), BF16),
            pltpu.VMEM(weight.shape, BF16),
            pltpu.VMEM(filt.shape, F32),
            pltpu.VMEM(rates.shape, F32),
        ],
        scratch_shapes=[pltpu.SemaphoreType.DMA((5,))],
        compiler_params=pltpu.CompilerParams(vmem_limit_bytes=4 * MIB),
        name="stage",
    )(ch, inputs[0], other, *inputs[1:])


def front_kernel(
    ch_ref,
    lhs_ref,
    halo_own_ref,
    halo_other_ref,
    w_ref,
    filt_ref,
    rates_ref,
    gain_ref,
    query_ref,
    local_ref,
    ends_ref,
    total_ref,
    halo_ref,
    proj_a,
    proj_b,
):
    rows = lhs_ref.shape[0]
    half = halo_own_ref.shape[1]
    steps = rows // SEGS
    pitch = steps + HISTORY
    modes = rates_ref.shape[0]
    streams = w_ref.shape[0]
    tiles = w_ref.shape[2] // WIDTH
    parts_of_rows = 2
    per = SEGS // parts_of_rows
    proj = (proj_a, proj_b)

    halo_ref[:, pl.ds(pl.multiple_of(ch_ref[0] * half, half), half)] = halo_own_ref[...]
    halo_ref[:, pl.ds(pl.multiple_of((1 - ch_ref[0]) * half, half), half)] = halo_other_ref[...]

    def projection(tile):
        held = proj[tile % 2]

        def piece(j, m):
            first = m * per
            lhs = lhs_ref[first * steps : (first + per) * steps]
            if m == 0:
                lhs = jnp.concatenate([halo_ref[...], lhs], axis=0)
            part = jnp.dot(
                lhs,
                w_ref[j, :, tile * WIDTH : (tile + 1) * WIDTH],
                preferred_element_type=F32,
            )
            for l in range(WIDTH // LANES):
                lanes = slice(l * LANES, (l + 1) * LANES)
                for g in range(first, first + per):
                    row = (g - first) * steps + (0 if m else HALO)
                    held[j, l, g * pitch + HISTORY : (g + 1) * pitch] = part[row : row + steps, lanes]
                    if g == 0:
                        held[j, l, :HISTORY] = part[row - HISTORY : row, lanes]
                    if g + 1 < SEGS:
                        held[j, l, (g + 1) * pitch : (g + 1) * pitch + HISTORY] = part[
                            row + steps - HISTORY : row + steps, lanes
                        ]

        return [lambda j=j, m=m: piece(j, m) for j in range(streams) for m in range(parts_of_rows)]

    def recurrence(tile, size=4):
        held = proj[tile % 2]
        pieces = []
        for l in range(WIDTH // LANES):
            lanes = slice(tile * WIDTH + l * LANES, tile * WIDTH + (l + 1) * LANES)
            kept = {}

            def at(j, t, l=l):
                return held[j, l, pl.ds(HISTORY + t, SEGS, stride=pitch), :]

            def begin(kept=kept, lanes=lanes, at=at):
                kept["taps"] = [
                    [spread(filt_ref[a, j : j + 1, lanes]) for a in range(3)] for j in range(streams)
                ]
                kept["decay"] = [spread(jnp.exp(-rates_ref[n : n + 1, lanes])) for n in range(modes)]
                kept["gain"] = [spread(gain_ref[n : n + 1, lanes]) for n in range(modes)]
                kept["one"] = [at(j, -1) for j in range(streams)]
                kept["two"] = [at(j, -2) for j in range(streams)]
                kept["state"] = [jnp.zeros((SEGS, LANES), F32)] * modes

            def advance(t0, kept=kept, lanes=lanes, at=at):
                for t in range(t0, t0 + size):
                    now = [at(j, t) for j in range(streams)]
                    q, k, v = [
                        filtered_step(*terms)
                        for terms in zip(kept["taps"], now, kept["one"], kept["two"])
                    ]
                    kept["one"], kept["two"] = now, kept["one"]
                    source = k * v
                    kept["state"] = [d * s + source for d, s in zip(kept["decay"], kept["state"])]
                    row = slice(t * SEGS, (t + 1) * SEGS)
                    query_ref[row, lanes] = q
                    local_ref[row, lanes] = tree_sum(
                        [g * s for g, s in zip(kept["gain"], kept["state"])]
                    )

            def finish(kept=kept, lanes=lanes):
                seg = lax.broadcasted_iota(jnp.int32, (SEGS, LANES), 0)
                later = (SEGS - 1 - seg).astype(F32) * float(steps)
                for n, state in enumerate(kept["state"]):
                    ends_ref[n * SEGS : (n + 1) * SEGS, lanes] = state
                    weight = jnp.exp(-spread(rates_ref[n : n + 1, lanes]) * later)
                    total_ref[n : n + 1, lanes] = jnp.sum(state * weight, axis=0, keepdims=True)

            pieces += [begin]
            pieces += [lambda t0=t0, advance=advance: advance(t0) for t0 in range(0, steps, size)]
            pieces += [finish]
        return pieces

    for work in projection(0):
        work()
    for tile in range(tiles):
        slow = projection(tile + 1) if tile + 1 < tiles else [lambda: None]
        fast = recurrence(tile)
        done = 0
        for i, work in enumerate(slow):
            work()
            upto = (i + 1) * len(fast) // len(slow)
            for step in fast[done:upto]:
                step()
            done = upto


def front_call(ch, lhs, halo_own, halo_other, weight, filt, rates, gain):
    rows, full = lhs.shape
    streams, _, channels = weight.shape
    modes = rates.shape[0]
    vmem = pl.BlockSpec(memory_space=pltpu.VMEM)
    held = pltpu.VMEM((streams, WIDTH // LANES, rows + SEGS * HISTORY, LANES), F32)
    return pl.pallas_call(
        front_kernel,
        in_specs=[pl.BlockSpec(memory_space=pltpu.SMEM)] + [vmem] * 7,
        out_specs=[vmem] * 4,
        out_shape=[
            pltpu.VMEM((rows, channels), F32),
            pltpu.VMEM((rows, channels), F32),
            pltpu.VMEM((modes * SEGS, channels), F32),
            pltpu.VMEM((modes, channels), F32),
        ],
        scratch_shapes=[pltpu.VMEM((HALO, full), BF16), held, held],
        compiler_params=pltpu.CompilerParams(vmem_limit_bytes=16 * MIB),
        name="front",
    )(ch, lhs, halo_own, halo_other, weight, filt, rates, gain)


def hidden_kernel(ends_ref, into_ref, local_ref, query_ref, rates_ref, gain_ref, hidden_ref):
    rows, channels = local_ref.shape
    steps = rows // SEGS
    modes = rates_ref.shape[0]
    seg = lax.broadcasted_iota(jnp.int32, (SEGS, LANES), 0)
    for i in range(channels // LANES):
        lanes = slice(i * LANES, (i + 1) * LANES)
        decays, leads = [], []
        for n in range(modes):
            rate = spread(rates_ref[n : n + 1, lanes])
            state = pltpu.roll(ends_ref[n * SEGS : (n + 1) * SEGS, lanes], 1, 0)
            state = jnp.where(seg == 0, spread(into_ref[n : n + 1, lanes]), state)
            for hop in (1, 2, 4):
                earlier = pltpu.roll(state, hop, 0) * jnp.exp(-rate * float(steps * hop))
                state = state + jnp.where(seg >= hop, earlier, 0.0)
            decays.append(jnp.exp(-rate))
            leads.append(spread(gain_ref[n : n + 1, lanes]) * state)

        def body(t, leads, lanes=lanes, decays=decays):
            halves = []
            for u in range(2):
                row = pl.ds(pl.multiple_of((2 * t + u) * SEGS, SEGS), SEGS)
                leads = tuple(d * s for d, s in zip(decays, leads))
                halves.append(query_ref[row, lanes] * (local_ref[row, lanes] + tree_sum(leads)))
            row = pl.ds(pl.multiple_of(2 * t * SEGS, 2 * SEGS), 2 * SEGS)
            hidden_ref[row, lanes] = jnp.concatenate(halves, axis=0).astype(BF16)
            return leads

        lax.fori_loop(0, steps // 2, body, tuple(leads), unroll=8)


def hidden_call(ends, into, local, query, rates, gain):
    vmem = pl.BlockSpec(memory_space=pltpu.VMEM)
    args = [pltpu.with_memory_space_constraint(x, pltpu.VMEM) for x in (ends, into, local, query, rates, gain)]
    return pl.pallas_call(
        hidden_kernel,
        in_specs=[vmem] * 6,
        out_specs=vmem,
        out_shape=pltpu.VMEM(local.shape, BF16),
        compiler_params=pltpu.CompilerParams(vmem_limit_bytes=4 * MIB),
        name="hidden",
    )(*args)


def product_kernel(ch_ref, hidden_ref, w_ref, out_ref):
    out_ref[...] = jnp.dot(hidden_ref[...], w_ref[...], preferred_element_type=F32)


def product_call(ch, hidden, weight, width=256):
    rows, channels = hidden.shape
    columns = weight.shape[1] // 2
    tiles = columns // width
    grid_spec = pltpu.PrefetchScalarGridSpec(
        num_scalar_prefetch=1,
        grid=(tiles,),
        in_specs=[
            pl.BlockSpec((rows, channels), lambda i, c: (0, 0)),
            pl.BlockSpec((channels, width), lambda i, c: (0, c[0] * tiles + i)),
        ],
        out_specs=pl.BlockSpec((rows, width), lambda i, c: (0, i)),
    )
    return pl.pallas_call(
        product_kernel,
        grid_spec=grid_spec,
        out_shape=jax.ShapeDtypeStruct((rows, columns), F32),
        compiler_params=pltpu.CompilerParams(vmem_limit_bytes=8 * MIB),
        name="product",
    )(ch, hidden, weight)


def output_kernel(ch_ref, part_ref, other_ref, w_ref, out_ref, acc_ref):
    rows, width = out_ref.shape
    steps = rows // SEGS
    part = part_ref[...] + jnp.dot(other_ref[...], w_ref[...], preferred_element_type=F32)
    for i in range(width // LANES):
        acc_ref[i] = part[:, i * LANES : (i + 1) * LANES]
    for i in range(width // LANES):
        for j in range(SEGS):
            out_ref[j * steps : (j + 1) * steps, i * LANES : (i + 1) * LANES] = acc_ref[
                i, pl.ds(j, steps, stride=SEGS), :
            ]


def output_call(ch, part, other, weight, width=256):
    rows, channels = other.shape
    columns = part.shape[1]
    tiles = columns // width
    grid_spec = pltpu.PrefetchScalarGridSpec(
        num_scalar_prefetch=1,
        grid=(tiles,),
        in_specs=[
            pl.BlockSpec((rows, width), lambda i, c: (0, i)),
            pl.BlockSpec((rows, channels), lambda i, c: (0, 0)),
            pl.BlockSpec((channels, width), lambda i, c: (0, c[0] * tiles + i)),
        ],
        out_specs=pl.BlockSpec((rows, width), lambda i, c: (0, i)),
        scratch_shapes=[pltpu.VMEM((width // LANES, rows, LANES), F32)],
    )
    return pl.pallas_call(
        output_kernel,
        grid_spec=grid_spec,
        out_shape=jax.ShapeDtypeStruct((rows, columns), F32),
        compiler_params=pltpu.CompilerParams(vmem_limit_bytes=8 * MIB),
        name="output",
    )(ch, part, other, weight)


def swapped(x):
    return lax.ppermute(x, "ch", [(0, 1), (1, 0)])


def from_before(x):
    count = RING**3
    return lax.ppermute(x, SEQ, [(i, i + 1) for i in range(count - 1)])


def ring_level(state, axis, rates, tokens):
    here = lax.axis_index(axis)
    sent = state.astype(BF16)
    arrived = [
        lax.ppermute(sent, axis, [(i, (i + k) % RING) for i in range(RING)]).astype(F32)
        for k in range(1, RING)
    ]
    before = jnp.zeros_like(state)
    total = state * jnp.exp(-rates * (tokens * (RING - 1 - here)).astype(F32))
    for k, part in zip(range(1, RING), arrived):
        weight = jnp.where(k <= here, jnp.exp(-rates * float(tokens * (k - 1))), 0.0)
        before = before + weight * part
        place = (here - k) % RING
        total = total + part * jnp.exp(-rates * (tokens * (RING - 1 - place)).astype(F32))
    return before, total


def on_device(tokens, in_weight, short_filter, residues, rates, out_weight):
    rows = tokens.shape[0]
    ch = lax.axis_index("ch").astype(jnp.int32).reshape(1)
    weight = in_weight.transpose(1, 0, 2)
    rates = rates.T
    gain = residues.T * jnp.sqrt(1.0 - jnp.exp(-2.0 * rates))

    halo_own = from_before(tokens[rows - HALO :])
    lhs, weight, filt, rates = stage_call(
        ch, tokens, swapped(tokens), weight, short_filter, rates
    )
    halo_own, lhs = lax.optimization_barrier((halo_own, lhs))
    halo_other = swapped(halo_own)
    out_weight_other = swapped(out_weight)
    query, local, ends, total = front_call(
        ch, lhs, halo_own, halo_other, weight, filt, rates, gain
    )

    into = jnp.zeros_like(total)
    after = 0
    span = rows
    for axis in reversed(SEQ):
        before, total = ring_level(total, axis, rates, span)
        into = into + before * jnp.exp(-rates * jnp.asarray(after, F32))
        after = after + span * lax.axis_index(axis)
        span = span * RING

    hidden = hidden_call(ends, into, local, query, rates, gain)
    part = product_call(ch, hidden, out_weight)
    return output_call(ch, part, swapped(hidden), out_weight_other)


def solution(mesh):
    cube = Mesh(mesh.devices.reshape(RING, RING, RING, 2), (*SEQ, "ch"))
    return jax.shard_map(
        on_device,
        mesh=cube,
        in_specs=(
            P(SEQ, "ch"),
            P(None, None, "ch"),
            P(None, None, "ch"),
            P("ch", None),
            P("ch", None),
            P("ch", None),
        ),
        out_specs=P(SEQ, "ch"),
        check_vma=False,
    )
```

```python
import jax
import jax.numpy as jnp
from jax import lax
from jax.experimental import pallas as pl
from jax.experimental.pallas import tpu as pltpu
from jax.sharding import Mesh, PartitionSpec as P

SEGS = 8
HALO = 16
LANES = 128
HISTORY = 8
WIDTH = 256
AHEAD = 2
SEQ = ("z", "y", "x")
RING = 4
F32 = jnp.float32
BF16 = jnp.bfloat16
MIB = 1024 * 1024


def spread(row):
    return jnp.broadcast_to(row, (SEGS, row.shape[-1]))


def filtered_step(taps, now, one, two):
    return taps[0] * now + taps[1] * one + taps[2] * two


def tree_sum(parts):
    parts = list(parts)
    while len(parts) > 1:
        parts = [a + b for a, b in zip(parts[::2], parts[1::2])]
    return parts[0]


def stage_kernel(
    where_ref,
    own_ref,
    other_ref,
    w_ref,
    filt_ref,
    rates_ref,
    lhs_out,
    w_out,
    filt_out,
    rates_out,
    into_out,
    total_out,
    sems,
):
    rows, half = own_ref.shape
    core = lax.rem(where_ref[0], 2)
    mine = pl.multiple_of(core * half, half)
    theirs = pl.multiple_of((1 - core) * half, half)
    pairs = [
        (rates_ref, rates_out),
        (own_ref, lhs_out.at[:, pl.ds(mine, half)]),
        (other_ref, lhs_out.at[:, pl.ds(theirs, half)]),
        (filt_ref, filt_out),
        (w_ref.at[:, :, pl.ds(0, w_out.shape[2])], w_out),
    ]
    copies = [pltpu.make_async_copy(src, dst, sems.at[i]) for i, (src, dst) in enumerate(pairs)]
    for copy in copies:
        copy.start()
    copies[0].wait()
    rates = rates_out[...]
    rest, span, after = where_ref[0] // 2, rows, 0

    def decay(tokens):
        return jnp.exp(-rates * jnp.asarray(tokens, F32))

    for level in range(len(SEQ)):
        here = lax.rem(rest, RING)
        rest = rest // RING
        total_out[RING * level] = decay(span * (RING - 1 - here))
        for k in range(1, RING):
            inside = (k <= here).astype(F32)
            into_out[(RING - 1) * level + k - 1] = inside * decay(span * (k - 1) + after)
            place = lax.rem(here - k + RING, RING)
            total_out[RING * level + k] = decay(span * (RING - 1 - place))
        after = after + span * here
        span = span * RING
    for copy in copies[1:]:
        copy.wait()


def stage_call(where, own, other, weight, filt, rates):
    rows, half = own.shape
    vmem = pl.BlockSpec(memory_space=pltpu.VMEM)
    anywhere = pl.BlockSpec(memory_space=pl.ANY)
    inputs = [pltpu.with_memory_space_constraint(x, pltpu.HBM) for x in (own, weight, filt, rates)]
    return pl.pallas_call(
        stage_kernel,
        in_specs=[pl.BlockSpec(memory_space=pltpu.SMEM)] + [anywhere] * 5,
        out_specs=[vmem] * 6,
        out_shape=[
            pltpu.VMEM((rows, 2 * half), BF16),
            pltpu.VMEM((*weight.shape[:2], AHEAD * WIDTH), BF16),
            pltpu.VMEM(filt.shape, F32),
            pltpu.VMEM(rates.shape, F32),
            pltpu.VMEM((len(SEQ) * (RING - 1), *rates.shape), F32),
            pltpu.VMEM((len(SEQ) * RING, *rates.shape), F32),
        ],
        scratch_shapes=[pltpu.SemaphoreType.DMA((5,))],
        compiler_params=pltpu.CompilerParams(vmem_limit_bytes=4 * MIB),
        name="stage",
    )(where, inputs[0], other, *inputs[1:])


def front_kernel(
    where_ref,
    lhs_ref,
    halo_own_ref,
    halo_other_ref,
    ahead_ref,
    w_ref,
    filt_ref,
    rates_ref,
    gain_ref,
    pair_ref,
    ends_ref,
    total_ref,
    halo_ref,
    rest_ref,
    proj_a,
    proj_b,
    sem,
):
    rows = lhs_ref.shape[0]
    half = halo_own_ref.shape[1]
    steps = rows // SEGS
    pitch = steps + HISTORY
    modes = rates_ref.shape[0]
    streams = w_ref.shape[0]
    tiles = w_ref.shape[2] // WIDTH
    parts_of_rows = 2
    per = SEGS // parts_of_rows
    proj = (proj_a, proj_b)

    rest = pltpu.make_async_copy(
        w_ref.at[:, :, pl.ds(AHEAD * WIDTH, (tiles - AHEAD) * WIDTH)], rest_ref, sem
    )
    rest.start()
    core = lax.rem(where_ref[0], 2)
    halo_ref[:, pl.ds(pl.multiple_of(core * half, half), half)] = halo_own_ref[...]
    halo_ref[:, pl.ds(pl.multiple_of((1 - core) * half, half), half)] = halo_other_ref[...]

    def projection(tile):
        held = proj[tile % 2]
        weights, column = (ahead_ref, tile) if tile < AHEAD else (rest_ref, tile - AHEAD)
        if tile == AHEAD:
            rest.wait()

        def piece(j, m):
            first = m * per
            lhs = lhs_ref[first * steps : (first + per) * steps]
            if m == 0:
                lhs = jnp.concatenate([halo_ref[...], lhs], axis=0)
            part = jnp.dot(
                lhs,
                weights[j, :, column * WIDTH : (column + 1) * WIDTH],
                preferred_element_type=F32,
            )
            for l in range(WIDTH // LANES):
                lanes = slice(l * LANES, (l + 1) * LANES)
                for g in range(first, first + per):
                    row = (g - first) * steps + (0 if m else HALO)
                    held[j, l, g * pitch + HISTORY : (g + 1) * pitch] = part[row : row + steps, lanes]
                    if g == 0:
                        held[j, l, :HISTORY] = part[row - HISTORY : row, lanes]
                    if g + 1 < SEGS:
                        held[j, l, (g + 1) * pitch : (g + 1) * pitch + HISTORY] = part[
                            row + steps - HISTORY : row + steps, lanes
                        ]

        return [lambda j=j, m=m: piece(j, m) for j in range(streams) for m in range(parts_of_rows)]

    def recurrence(tile, size=4):
        held = proj[tile % 2]
        pieces = []
        for l in range(WIDTH // LANES):
            lanes = slice(tile * WIDTH + l * LANES, tile * WIDTH + (l + 1) * LANES)
            kept = {}

            def at(j, t, l=l):
                return held[j, l, pl.ds(HISTORY + t, SEGS, stride=pitch), :]

            def begin(kept=kept, lanes=lanes, at=at):
                kept["taps"] = [
                    [spread(filt_ref[a, j : j + 1, lanes]) for a in range(3)] for j in range(streams)
                ]
                kept["decay"] = [spread(jnp.exp(-rates_ref[n : n + 1, lanes])) for n in range(modes)]
                kept["gain"] = [spread(gain_ref[n : n + 1, lanes]) for n in range(modes)]
                kept["one"] = [at(j, -1) for j in range(streams)]
                kept["two"] = [at(j, -2) for j in range(streams)]
                kept["state"] = [jnp.zeros((SEGS, LANES), F32)] * modes

            def advance(t0, kept=kept, lanes=lanes, at=at):
                for t in range(t0, t0 + size):
                    now = [at(j, t) for j in range(streams)]
                    q, k, v = [
                        filtered_step(*terms)
                        for terms in zip(kept["taps"], now, kept["one"], kept["two"])
                    ]
                    kept["one"], kept["two"] = now, kept["one"]
                    source = k * v
                    kept["state"] = [d * s + source for d, s in zip(kept["decay"], kept["state"])]
                    row = slice(t * SEGS, (t + 1) * SEGS)
                    pair_ref[0, row, lanes] = q
                    pair_ref[1, row, lanes] = tree_sum(
                        [g * s for g, s in zip(kept["gain"], kept["state"])]
                    )

            def finish(kept=kept, lanes=lanes):
                seg = lax.broadcasted_iota(jnp.int32, (SEGS, LANES), 0)
                later = (SEGS - 1 - seg).astype(F32) * float(steps)
                for n, state in enumerate(kept["state"]):
                    ends_ref[n * SEGS : (n + 1) * SEGS, lanes] = state
                    weight = jnp.exp(-spread(rates_ref[n : n + 1, lanes]) * later)
                    total_ref[n : n + 1, lanes] = jnp.sum(state * weight, axis=0, keepdims=True)

            pieces += [begin]
            pieces += [lambda t0=t0, advance=advance: advance(t0) for t0 in range(0, steps, size)]
            pieces += [finish]
        return pieces

    for work in projection(0):
        work()
    for tile in range(tiles):
        slow = projection(tile + 1) if tile + 1 < tiles else [lambda: None]
        fast = recurrence(tile)
        done = 0
        for i, work in enumerate(slow):
            work()
            upto = (i + 1) * len(fast) // len(slow)
            for step in fast[done:upto]:
                step()
            done = upto


def front_call(where, lhs, halo_own, halo_other, ahead, weight, filt, rates, gain):
    rows, full = lhs.shape
    streams, _, channels = weight.shape
    modes = rates.shape[0]
    vmem = pl.BlockSpec(memory_space=pltpu.VMEM)
    held = pltpu.VMEM((streams, WIDTH // LANES, rows + SEGS * HISTORY, LANES), F32)
    return pl.pallas_call(
        front_kernel,
        in_specs=[pl.BlockSpec(memory_space=pltpu.SMEM)]
        + [vmem] * 4
        + [pl.BlockSpec(memory_space=pl.ANY)]
        + [vmem] * 3,
        out_specs=[vmem] * 3,
        out_shape=[
            pltpu.VMEM((2, rows, channels), F32),
            pltpu.VMEM((modes * SEGS, channels), F32),
            pltpu.VMEM((modes, channels), F32),
        ],
        scratch_shapes=[
            pltpu.VMEM((HALO, full), BF16),
            pltpu.VMEM((streams, full, channels - AHEAD * WIDTH), BF16),
            held,
            held,
            pltpu.SemaphoreType.DMA,
        ],
        compiler_params=pltpu.CompilerParams(vmem_limit_bytes=18 * MIB),
        name="front",
    )(
        where,
        lhs,
        halo_own,
        halo_other,
        ahead,
        pltpu.with_memory_space_constraint(weight, pltpu.HBM),
        filt,
        rates,
        gain,
    )


def hidden_kernel(ends_ref, into_ref, pair_ref, rates_ref, gain_ref, hidden_ref):
    _, rows, channels = pair_ref.shape
    steps = rows // SEGS
    modes = rates_ref.shape[0]
    seg = lax.broadcasted_iota(jnp.int32, (SEGS, LANES), 0)
    for i in range(channels // LANES):
        lanes = slice(i * LANES, (i + 1) * LANES)
        decays, leads = [], []
        for n in range(modes):
            rate = spread(rates_ref[n : n + 1, lanes])
            state = pltpu.roll(ends_ref[n * SEGS : (n + 1) * SEGS, lanes], 1, 0)
            state = jnp.where(seg == 0, spread(into_ref[n : n + 1, lanes]), state)
            for hop in (1, 2, 4):
                earlier = pltpu.roll(state, hop, 0) * jnp.exp(-rate * float(steps * hop))
                state = state + jnp.where(seg >= hop, earlier, 0.0)
            decays.append(jnp.exp(-rate))
            leads.append(spread(gain_ref[n : n + 1, lanes]) * state)

        def body(t, leads, lanes=lanes, decays=decays):
            halves = []
            for u in range(2):
                row = pl.ds(pl.multiple_of((2 * t + u) * SEGS, SEGS), SEGS)
                leads = tuple(d * s for d, s in zip(decays, leads))
                halves.append(pair_ref[0, row, lanes] * (pair_ref[1, row, lanes] + tree_sum(leads)))
            row = pl.ds(pl.multiple_of(2 * t * SEGS, 2 * SEGS), 2 * SEGS)
            hidden_ref[row, lanes] = jnp.concatenate(halves, axis=0).astype(BF16)
            return leads

        lax.fori_loop(0, steps // 2, body, tuple(leads), unroll=8)


def hidden_call(ends, into, pair, rates, gain):
    vmem = pl.BlockSpec(memory_space=pltpu.VMEM)
    args = [pltpu.with_memory_space_constraint(x, pltpu.VMEM) for x in (ends, into, pair, rates, gain)]
    return pl.pallas_call(
        hidden_kernel,
        in_specs=[vmem] * 5,
        out_specs=vmem,
        out_shape=pltpu.VMEM(pair.shape[1:], BF16),
        compiler_params=pltpu.CompilerParams(vmem_limit_bytes=4 * MIB),
        name="hidden",
    )(*args)


def product_kernel(where_ref, hidden_ref, w_ref, w_other_ref, part_ref, staged_ref, mine_ref, sems):
    columns = part_ref.shape[1]
    lanes = pl.ds(pl.multiple_of(lax.rem(where_ref[0], 2) * columns, columns), columns)
    mine = pltpu.make_async_copy(w_ref.at[:, lanes], mine_ref, sems.at[0])
    theirs = pltpu.make_async_copy(w_other_ref.at[:, lanes], staged_ref, sems.at[1])
    mine.start()
    theirs.start()
    mine.wait()
    part_ref[...] = jnp.dot(hidden_ref[...], mine_ref[...], preferred_element_type=F32)
    theirs.wait()


def product_call(where, hidden, weight, weight_other):
    rows, channels = hidden.shape
    columns = weight.shape[1] // 2
    vmem = pl.BlockSpec(memory_space=pltpu.VMEM)
    anywhere = pl.BlockSpec(memory_space=pl.ANY)
    return pl.pallas_call(
        product_kernel,
        in_specs=[pl.BlockSpec(memory_space=pltpu.SMEM), vmem, anywhere, anywhere],
        out_specs=[vmem] * 2,
        out_shape=[pltpu.VMEM((rows, columns), F32), pltpu.VMEM((channels, columns), BF16)],
        scratch_shapes=[pltpu.VMEM((channels, columns), BF16), pltpu.SemaphoreType.DMA((2,))],
        compiler_params=pltpu.CompilerParams(vmem_limit_bytes=8 * MIB),
        name="product",
    )(where, hidden, weight, weight_other)


def output_kernel(part_ref, other_ref, w_ref, out_ref, acc_ref, rows_ref, sems):
    rows, columns = part_ref.shape
    steps = rows // SEGS
    copies = []
    for tile in range(columns // WIDTH):
        lanes = slice(tile * WIDTH, (tile + 1) * WIDTH)
        part = part_ref[:, lanes] + jnp.dot(
            other_ref[...], w_ref[:, lanes], preferred_element_type=F32
        )
        for l in range(WIDTH // LANES):
            acc_ref[tile, l] = part[:, l * LANES : (l + 1) * LANES]
            for j in range(SEGS):
                rows_ref[
                    j * steps : (j + 1) * steps,
                    tile * WIDTH + l * LANES : tile * WIDTH + (l + 1) * LANES,
                ] = acc_ref[tile, l, pl.ds(j, steps, stride=SEGS), :]
        copies.append(pltpu.make_async_copy(rows_ref.at[:, lanes], out_ref.at[:, lanes], sems.at[tile]))
        copies[-1].start()
    for copy in copies:
        copy.wait()


def output_call(part, other, weight):
    rows, columns = part.shape
    vmem = pl.BlockSpec(memory_space=pltpu.VMEM)
    args = [pltpu.with_memory_space_constraint(x, pltpu.VMEM) for x in (part, other, weight)]
    return pl.pallas_call(
        output_kernel,
        in_specs=[vmem] * 3,
        out_specs=pl.BlockSpec(memory_space=pl.ANY),
        out_shape=jax.ShapeDtypeStruct((rows, columns), F32),
        scratch_shapes=[
            pltpu.VMEM((columns // WIDTH, WIDTH // LANES, rows, LANES), F32),
            pltpu.VMEM((rows, columns), F32),
            pltpu.SemaphoreType.DMA((columns // WIDTH,)),
        ],
        compiler_params=pltpu.CompilerParams(vmem_limit_bytes=8 * MIB),
        name="output",
    )(*args)


def swapped(x):
    return lax.ppermute(x, "ch", [(0, 1), (1, 0)])


def from_before(x):
    count = RING**3
    return lax.ppermute(x, SEQ, [(i, i + 1) for i in range(count - 1)])


def round_the_ring(state, axis):
    sent = state.astype(BF16)
    return [
        lax.ppermute(sent, axis, [(i, (i + k) % RING) for i in range(RING)]).astype(F32)
        for k in range(1, RING)
    ]


def on_device(tokens, in_weight, short_filter, residues, rates, out_weight):
    rows = tokens.shape[0]
    where = lax.axis_index((*SEQ, "ch")).astype(jnp.int32).reshape(1)
    weight = in_weight.transpose(1, 0, 2)
    rates = rates.T
    gain = residues.T * jnp.sqrt(1.0 - jnp.exp(-2.0 * rates))

    halo_own = from_before(tokens[rows - HALO :])
    lhs, ahead, filt, rates, into_weights, total_weights = stage_call(
        where, tokens, swapped(tokens), weight, short_filter, rates
    )
    halo_own, lhs, out_weight = lax.optimization_barrier((halo_own, lhs, out_weight))
    halo_other = swapped(halo_own)
    lhs, halo_other, out_weight = lax.optimization_barrier((lhs, halo_other, out_weight))
    out_weight_other = swapped(out_weight)
    pair, ends, total = front_call(
        where, lhs, halo_own, halo_other, ahead, weight, filt, rates, gain
    )

    into = 0.0
    for level, axis in enumerate(reversed(SEQ)):
        arrived = round_the_ring(total, axis)
        total = total_weights[RING * level] * total
        for k, part in enumerate(arrived):
            into = into + into_weights[(RING - 1) * level + k] * part
            total = total + total_weights[RING * level + k + 1] * part

    hidden = hidden_call(ends, into, pair, rates, gain)
    part, staged = product_call(where, hidden, out_weight, out_weight_other)
    return output_call(part, swapped(hidden), staged)


def solution(mesh):
    cube = Mesh(mesh.devices.reshape(RING, RING, RING, 2), (*SEQ, "ch"))
    return jax.shard_map(
        on_device,
        mesh=cube,
        in_specs=(
            P(SEQ, "ch"),
            P(None, None, "ch"),
            P(None, None, "ch"),
            P("ch", None),
            P("ch", None),
            P("ch", None),
        ),
        out_specs=P(SEQ, "ch"),
        check_vma=False,
    )
```

```python
import jax
import jax.numpy as jnp
from jax import lax
from jax.experimental import pallas as pl
from jax.experimental.pallas import tpu as pltpu
from jax.sharding import Mesh, PartitionSpec as P

SEGS = 8
HALO = 16
LANES = 128
HISTORY = 8
WIDTH = 256
SEQ = ("z", "y", "x")
RING = 4
F32 = jnp.float32
BF16 = jnp.bfloat16
MIB = 1024 * 1024


def spread(row):
    return jnp.broadcast_to(row, (SEGS, row.shape[-1]))


def filtered_step(taps, now, one, two):
    return taps[0] * now + taps[1] * one + taps[2] * two


def tree_sum(parts):
    parts = list(parts)
    while len(parts) > 1:
        parts = [a + b for a, b in zip(parts[::2], parts[1::2])]
    return parts[0]


def stage_kernel(
    where_ref,
    own_ref,
    other_ref,
    w_ref,
    filt_ref,
    rates_ref,
    lhs_out,
    w_out,
    filt_out,
    rates_out,
    into_out,
    total_out,
    sems,
):
    rows, half = own_ref.shape
    core = lax.rem(where_ref[0], 2)
    mine = pl.multiple_of(core * half, half)
    theirs = pl.multiple_of((1 - core) * half, half)
    pairs = [
        (rates_ref, rates_out),
        (own_ref, lhs_out.at[:, pl.ds(mine, half)]),
        (other_ref, lhs_out.at[:, pl.ds(theirs, half)]),
        (filt_ref, filt_out),
        (w_ref.at[pl.ds(1, w_out.shape[0])], w_out),
    ]
    copies = [pltpu.make_async_copy(src, dst, sems.at[i]) for i, (src, dst) in enumerate(pairs)]
    for copy in copies:
        copy.start()
    copies[0].wait()
    rates = rates_out[...]
    rest, span, after = where_ref[0] // 2, rows, 0

    def decay(tokens):
        return jnp.exp(-rates * jnp.asarray(tokens, F32))

    for level in range(len(SEQ)):
        here = lax.rem(rest, RING)
        rest = rest // RING
        total_out[RING * level] = decay(span * (RING - 1 - here))
        for k in range(1, RING):
            inside = (k <= here).astype(F32)
            into_out[(RING - 1) * level + k - 1] = inside * decay(span * (k - 1) + after)
            place = lax.rem(here - k + RING, RING)
            total_out[RING * level + k] = decay(span * (RING - 1 - place))
        after = after + span * here
        span = span * RING
    for copy in copies[1:]:
        copy.wait()


def stage_call(where, own, other, weight, filt, rates):
    rows, half = own.shape
    vmem = pl.BlockSpec(memory_space=pltpu.VMEM)
    anywhere = pl.BlockSpec(memory_space=pl.ANY)
    inputs = [pltpu.with_memory_space_constraint(x, pltpu.HBM) for x in (own, weight, filt, rates)]
    return pl.pallas_call(
        stage_kernel,
        in_specs=[pl.BlockSpec(memory_space=pltpu.SMEM)] + [anywhere] * 5,
        out_specs=[vmem] * 6,
        out_shape=[
            pltpu.VMEM((rows, 2 * half), BF16),
            pltpu.VMEM((weight.shape[0] - 1, *weight.shape[1:]), BF16),
            pltpu.VMEM(filt.shape, F32),
            pltpu.VMEM(rates.shape, F32),
            pltpu.VMEM((len(SEQ) * (RING - 1), *rates.shape), F32),
            pltpu.VMEM((len(SEQ) * RING, *rates.shape), F32),
        ],
        scratch_shapes=[pltpu.SemaphoreType.DMA((5,))],
        compiler_params=pltpu.CompilerParams(vmem_limit_bytes=4 * MIB),
        name="stage",
    )(where, inputs[0], other, *inputs[1:])


def hold_segments(held, part, first, per):
    steps = held.shape[1] // SEGS - HISTORY
    pitch = steps + HISTORY
    for l in range(WIDTH // LANES):
        lanes = slice(l * LANES, (l + 1) * LANES)
        for g in range(first, first + per):
            row = (g - first) * steps + (0 if first else HALO)
            held[l, g * pitch + HISTORY : (g + 1) * pitch] = part[row : row + steps, lanes]
            if g == 0:
                held[l, :HISTORY] = part[row - HISTORY : row, lanes]
            if g + 1 < SEGS:
                held[l, (g + 1) * pitch : (g + 1) * pitch + HISTORY] = part[
                    row + steps - HISTORY : row + steps, lanes
                ]


def join_halo(where_ref, halo_ref, own_ref, other_ref):
    half = own_ref.shape[1]
    core = lax.rem(where_ref[0], 2)
    halo_ref[:, pl.ds(pl.multiple_of(core * half, half), half)] = own_ref[...]
    halo_ref[:, pl.ds(pl.multiple_of((1 - core) * half, half), half)] = other_ref[...]


def segment_rows(lhs_ref, halo_ref, first, per):
    steps = lhs_ref.shape[0] // SEGS
    rows = lhs_ref[first * steps : (first + per) * steps]
    return rows if first else jnp.concatenate([halo_ref[...], rows], axis=0)


def front_kernel(
    where_ref,
    lhs_ref,
    halo_own_ref,
    halo_other_ref,
    w_ref,
    wq_ref,
    filt_ref,
    rates_ref,
    gain_ref,
    local_ref,
    ends_ref,
    total_ref,
    staged_ref,
    halo_ref,
    proj_a,
    proj_b,
    sem,
):
    rows = lhs_ref.shape[0]
    steps = rows // SEGS
    pitch = steps + HISTORY
    modes = rates_ref.shape[0]
    streams = w_ref.shape[0]
    tiles = w_ref.shape[2] // WIDTH
    per = SEGS // 2
    proj = (proj_a, proj_b)

    stage = pltpu.make_async_copy(wq_ref.at[0], staged_ref, sem)
    stage.start()
    join_halo(where_ref, halo_ref, halo_own_ref, halo_other_ref)

    def projection(tile):
        held = proj[tile % 2]

        def piece(j, first):
            part = jnp.dot(
                segment_rows(lhs_ref, halo_ref, first, per),
                w_ref[j, :, tile * WIDTH : (tile + 1) * WIDTH],
                preferred_element_type=F32,
            )
            hold_segments(held.at[j], part, first, per)

        return [
            lambda j=j, first=first: piece(j, first)
            for j in range(streams)
            for first in range(0, SEGS, per)
        ]

    def recurrence(tile, size=4):
        held = proj[tile % 2]
        pieces = []
        for l in range(WIDTH // LANES):
            lanes = slice(tile * WIDTH + l * LANES, tile * WIDTH + (l + 1) * LANES)
            kept = {}

            def at(j, t, l=l):
                return held[j, l, pl.ds(HISTORY + t, SEGS, stride=pitch), :]

            def begin(kept=kept, lanes=lanes, at=at):
                kept["taps"] = [
                    [spread(filt_ref[a, j + 1 : j + 2, lanes]) for a in range(3)]
                    for j in range(streams)
                ]
                kept["decay"] = [spread(jnp.exp(-rates_ref[n : n + 1, lanes])) for n in range(modes)]
                kept["gain"] = [spread(gain_ref[n : n + 1, lanes]) for n in range(modes)]
                kept["one"] = [at(j, -1) for j in range(streams)]
                kept["two"] = [at(j, -2) for j in range(streams)]
                kept["state"] = [jnp.zeros((SEGS, LANES), F32)] * modes

            def advance(t0, kept=kept, lanes=lanes, at=at):
                for t in range(t0, t0 + size):
                    now = [at(j, t) for j in range(streams)]
                    k, v = [
                        filtered_step(*terms)
                        for terms in zip(kept["taps"], now, kept["one"], kept["two"])
                    ]
                    kept["one"], kept["two"] = now, kept["one"]
                    source = k * v
                    kept["state"] = [d * s + source for d, s in zip(kept["decay"], kept["state"])]
                    local_ref[t * SEGS : (t + 1) * SEGS, lanes] = tree_sum(
                        [g * s for g, s in zip(kept["gain"], kept["state"])]
                    )

            def finish(kept=kept, lanes=lanes):
                seg = lax.broadcasted_iota(jnp.int32, (SEGS, LANES), 0)
                later = (SEGS - 1 - seg).astype(F32) * float(steps)
                for n, state in enumerate(kept["state"]):
                    ends_ref[n * SEGS : (n + 1) * SEGS, lanes] = state
                    weight = jnp.exp(-spread(rates_ref[n : n + 1, lanes]) * later)
                    total_ref[n : n + 1, lanes] = jnp.sum(state * weight, axis=0, keepdims=True)

            pieces += [begin]
            pieces += [lambda t0=t0, advance=advance: advance(t0) for t0 in range(0, steps, size)]
            pieces += [finish]
        return pieces

    for work in projection(0):
        work()
    for tile in range(tiles):
        slow = projection(tile + 1) if tile + 1 < tiles else [lambda: None]
        fast = recurrence(tile)
        done = 0
        for i, work in enumerate(slow):
            work()
            upto = (i + 1) * len(fast) // len(slow)
            for step in fast[done:upto]:
                step()
            done = upto
    stage.wait()


def front_call(where, lhs, halo_own, halo_other, staged, weight, filt, rates, gain):
    rows, full = lhs.shape
    streams, _, channels = staged.shape
    modes = rates.shape[0]
    vmem = pl.BlockSpec(memory_space=pltpu.VMEM)
    held = pltpu.VMEM((streams, WIDTH // LANES, rows + SEGS * HISTORY, LANES), F32)
    return pl.pallas_call(
        front_kernel,
        in_specs=[pl.BlockSpec(memory_space=pltpu.SMEM)]
        + [vmem] * 4
        + [pl.BlockSpec(memory_space=pl.ANY)]
        + [vmem] * 3,
        out_specs=[vmem] * 4,
        out_shape=[
            pltpu.VMEM((rows, channels), F32),
            pltpu.VMEM((modes * SEGS, channels), F32),
            pltpu.VMEM((modes, channels), F32),
            pltpu.VMEM((full, channels), BF16),
        ],
        scratch_shapes=[pltpu.VMEM((HALO, full), BF16), held, held, pltpu.SemaphoreType.DMA],
        compiler_params=pltpu.CompilerParams(vmem_limit_bytes=10 * MIB),
        name="front",
    )(
        where,
        lhs,
        halo_own,
        halo_other,
        staged,
        pltpu.with_memory_space_constraint(weight, pltpu.HBM),
        filt,
        rates,
        gain,
    )


def query_kernel(where_ref, lhs_ref, halo_own_ref, halo_other_ref, w_ref, filt_ref, query_ref, halo_ref, held):
    steps = lhs_ref.shape[0] // SEGS
    pitch = steps + HISTORY
    per = SEGS // 2
    join_halo(where_ref, halo_ref, halo_own_ref, halo_other_ref)
    for tile in range(w_ref.shape[1] // WIDTH):
        for first in range(0, SEGS, per):
            part = jnp.dot(
                segment_rows(lhs_ref, halo_ref, first, per),
                w_ref[:, tile * WIDTH : (tile + 1) * WIDTH],
                preferred_element_type=F32,
            )
            hold_segments(held.at[tile], part, first, per)
        for l in range(WIDTH // LANES):
            lanes = slice(tile * WIDTH + l * LANES, tile * WIDTH + (l + 1) * LANES)
            taps = [spread(filt_ref[a, 0:1, lanes]) for a in range(3)]

            def at(t, tile=tile, l=l):
                return held[tile, l, pl.ds(HISTORY + t, SEGS, stride=pitch), :]

            one, two = at(-1), at(-2)
            for t in range(steps):
                now = at(t)
                query_ref[t * SEGS : (t + 1) * SEGS, lanes] = filtered_step(taps, now, one, two)
                one, two = now, one


def query_call(where, lhs, halo_own, halo_other, weight, filt):
    rows, full = lhs.shape
    channels = weight.shape[1]
    vmem = pl.BlockSpec(memory_space=pltpu.VMEM)
    args = [
        pltpu.with_memory_space_constraint(x, pltpu.VMEM)
        for x in (lhs, halo_own, halo_other, weight, filt)
    ]
    return pl.pallas_call(
        query_kernel,
        in_specs=[pl.BlockSpec(memory_space=pltpu.SMEM)] + [vmem] * 5,
        out_specs=vmem,
        out_shape=pltpu.VMEM((rows, channels), F32),
        scratch_shapes=[
            pltpu.VMEM((HALO, full), BF16),
            pltpu.VMEM((channels // WIDTH, WIDTH // LANES, rows + SEGS * HISTORY, LANES), F32),
        ],
        compiler_params=pltpu.CompilerParams(vmem_limit_bytes=6 * MIB),
        cost_estimate=pl.CostEstimate(
            flops=2 * (rows + HALO) * full * channels, transcendentals=0, bytes_accessed=0
        ),
        name="query",
    )(where, *args)


def hidden_kernel(ends_ref, into_ref, local_ref, query_ref, rates_ref, gain_ref, hidden_ref):
    rows, channels = local_ref.shape
    steps = rows // SEGS
    modes = rates_ref.shape[0]
    seg = lax.broadcasted_iota(jnp.int32, (SEGS, LANES), 0)
    for i in range(channels // LANES):
        lanes = slice(i * LANES, (i + 1) * LANES)
        decays, leads = [], []
        for n in range(modes):
            rate = spread(rates_ref[n : n + 1, lanes])
            state = pltpu.roll(ends_ref[n * SEGS : (n + 1) * SEGS, lanes], 1, 0)
            state = jnp.where(seg == 0, spread(into_ref[n : n + 1, lanes]), state)
            for hop in (1, 2, 4):
                earlier = pltpu.roll(state, hop, 0) * jnp.exp(-rate * float(steps * hop))
                state = state + jnp.where(seg >= hop, earlier, 0.0)
            decays.append(jnp.exp(-rate))
            leads.append(spread(gain_ref[n : n + 1, lanes]) * state)

        def body(t, leads, lanes=lanes, decays=decays):
            halves = []
            for u in range(2):
                row = pl.ds(pl.multiple_of((2 * t + u) * SEGS, SEGS), SEGS)
                leads = tuple(d * s for d, s in zip(decays, leads))
                halves.append(query_ref[row, lanes] * (local_ref[row, lanes] + tree_sum(leads)))
            row = pl.ds(pl.multiple_of(2 * t * SEGS, 2 * SEGS), 2 * SEGS)
            hidden_ref[row, lanes] = jnp.concatenate(halves, axis=0).astype(BF16)
            return leads

        lax.fori_loop(0, steps // 2, body, tuple(leads), unroll=8)


def hidden_call(ends, into, local, query, rates, gain):
    vmem = pl.BlockSpec(memory_space=pltpu.VMEM)
    args = [
        pltpu.with_memory_space_constraint(x, pltpu.VMEM)
        for x in (ends, into, local, query, rates, gain)
    ]
    return pl.pallas_call(
        hidden_kernel,
        in_specs=[vmem] * 6,
        out_specs=vmem,
        out_shape=pltpu.VMEM(local.shape, BF16),
        compiler_params=pltpu.CompilerParams(vmem_limit_bytes=4 * MIB),
        name="hidden",
    )(*args)


def product_kernel(where_ref, hidden_ref, w_ref, w_other_ref, part_ref, staged_ref, mine_ref, sems):
    columns = part_ref.shape[1]
    lanes = pl.ds(pl.multiple_of(lax.rem(where_ref[0], 2) * columns, columns), columns)
    mine = pltpu.make_async_copy(w_ref.at[:, lanes], mine_ref, sems.at[0])
    theirs = pltpu.make_async_copy(w_other_ref.at[:, lanes], staged_ref, sems.at[1])
    mine.start()
    theirs.start()
    mine.wait()
    part_ref[...] = jnp.dot(hidden_ref[...], mine_ref[...], preferred_element_type=F32)
    theirs.wait()


def product_call(where, hidden, weight, weight_other):
    rows, channels = hidden.shape
    columns = weight.shape[1] // 2
    vmem = pl.BlockSpec(memory_space=pltpu.VMEM)
    anywhere = pl.BlockSpec(memory_space=pl.ANY)
    return pl.pallas_call(
        product_kernel,
        in_specs=[pl.BlockSpec(memory_space=pltpu.SMEM), vmem, anywhere, anywhere],
        out_specs=[vmem] * 2,
        out_shape=[pltpu.VMEM((rows, columns), F32), pltpu.VMEM((channels, columns), BF16)],
        scratch_shapes=[pltpu.VMEM((channels, columns), BF16), pltpu.SemaphoreType.DMA((2,))],
        compiler_params=pltpu.CompilerParams(vmem_limit_bytes=8 * MIB),
        name="product",
    )(where, hidden, weight, weight_other)


def output_kernel(part_ref, other_ref, w_ref, out_ref, acc_ref, rows_ref, sems):
    rows, columns = part_ref.shape
    steps = rows // SEGS
    copies = []
    for tile in range(columns // WIDTH):
        lanes = slice(tile * WIDTH, (tile + 1) * WIDTH)
        part = part_ref[:, lanes] + jnp.dot(
            other_ref[...], w_ref[:, lanes], preferred_element_type=F32
        )
        for l in range(WIDTH // LANES):
            acc_ref[tile, l] = part[:, l * LANES : (l + 1) * LANES]
            for j in range(SEGS):
                rows_ref[
                    j * steps : (j + 1) * steps,
                    tile * WIDTH + l * LANES : tile * WIDTH + (l + 1) * LANES,
                ] = acc_ref[tile, l, pl.ds(j, steps, stride=SEGS), :]
        copies.append(pltpu.make_async_copy(rows_ref.at[:, lanes], out_ref.at[:, lanes], sems.at[tile]))
        copies[-1].start()
    for copy in copies:
        copy.wait()


def output_call(part, other, weight):
    rows, columns = part.shape
    vmem = pl.BlockSpec(memory_space=pltpu.VMEM)
    args = [pltpu.with_memory_space_constraint(x, pltpu.VMEM) for x in (part, other, weight)]
    return pl.pallas_call(
        output_kernel,
        in_specs=[vmem] * 3,
        out_specs=pl.BlockSpec(memory_space=pl.ANY),
        out_shape=jax.ShapeDtypeStruct((rows, columns), F32),
        scratch_shapes=[
            pltpu.VMEM((columns // WIDTH, WIDTH // LANES, rows, LANES), F32),
            pltpu.VMEM((rows, columns), F32),
            pltpu.SemaphoreType.DMA((columns // WIDTH,)),
        ],
        compiler_params=pltpu.CompilerParams(vmem_limit_bytes=8 * MIB),
        name="output",
    )(*args)


def swapped(x):
    return lax.ppermute(x, "ch", [(0, 1), (1, 0)])


def from_before(x):
    count = RING**3
    return lax.ppermute(x, SEQ, [(i, i + 1) for i in range(count - 1)])


def round_the_ring(state, axis):
    sent = state.astype(BF16)
    return [
        lax.ppermute(sent, axis, [(i, (i + k) % RING) for i in range(RING)])
        for k in range(1, RING)
    ]


def on_device(tokens, in_weight, short_filter, residues, rates, out_weight):
    rows = tokens.shape[0]
    where = lax.axis_index((*SEQ, "ch")).astype(jnp.int32).reshape(1)
    weight = in_weight.transpose(1, 0, 2)
    rates = rates.T
    gain = residues.T * jnp.sqrt(1.0 - jnp.exp(-2.0 * rates))

    halo_own = from_before(tokens[rows - HALO :])
    lhs, staged, filt, rates, into_weights, total_weights = stage_call(
        where, tokens, swapped(tokens), weight, short_filter, rates
    )
    halo_own, lhs, out_weight = lax.optimization_barrier((halo_own, lhs, out_weight))
    halo_other = swapped(halo_own)
    lhs, halo_other, out_weight = lax.optimization_barrier((lhs, halo_other, out_weight))
    out_weight_other = swapped(out_weight)
    local, ends, total, query_weight = front_call(
        where, lhs, halo_own, halo_other, staged, weight, filt, rates, gain
    )
    query = query_call(where, lhs, halo_own, halo_other, query_weight, filt)

    into = 0.0
    for level, axis in enumerate(reversed(SEQ)):
        arrived = round_the_ring(total, axis)
        if level == 0:
            query, *arrived = lax.optimization_barrier((query, *arrived))
        total = total_weights[RING * level] * total
        for k, part in enumerate(arrived):
            part = part.astype(F32)
            into = into + into_weights[(RING - 1) * level + k] * part
            total = total + total_weights[RING * level + k + 1] * part

    hidden = hidden_call(ends, into, local, query, rates, gain)
    part, partner_weight = product_call(where, hidden, out_weight, out_weight_other)
    return output_call(part, swapped(hidden), partner_weight)


def solution(mesh):
    cube = Mesh(mesh.devices.reshape(RING, RING, RING, 2), (*SEQ, "ch"))
    return jax.shard_map(
        on_device,
        mesh=cube,
        in_specs=(
            P(SEQ, "ch"),
            P(None, None, "ch"),
            P(None, None, "ch"),
            P("ch", None),
            P("ch", None),
            P("ch", None),
        ),
        out_specs=P(SEQ, "ch"),
        check_vma=False,
    )
```

```python
import functools

import jax
import jax.numpy as jnp
from jax import lax
from jax.experimental import pallas as pl
from jax.experimental.pallas import tpu as pltpu
from jax.sharding import Mesh, PartitionSpec as P

SEGS = 8
HALO = 16
LANES = 128
HISTORY = 8
WIDTH = 256
SEQ = ("z", "y", "x")
RING = 4
PARTS = 2
F32 = jnp.float32
BF16 = jnp.bfloat16
MIB = 1024 * 1024


def spread(row):
    return jnp.broadcast_to(row, (SEGS, row.shape[-1]))


def filtered_step(taps, now, one, two):
    return taps[0] * now + taps[1] * one + taps[2] * two


def tree_sum(parts):
    parts = list(parts)
    while len(parts) > 1:
        parts = [a + b for a, b in zip(parts[::2], parts[1::2])]
    return parts[0]


def stage_kernel(
    where_ref,
    own_ref,
    other_ref,
    w_ref,
    filt_ref,
    rates_ref,
    lhs_out,
    w_out,
    filt_out,
    rates_out,
    into_out,
    total_out,
    sems,
):
    rows, half = own_ref.shape
    core = lax.rem(where_ref[0], 2)
    mine = pl.multiple_of(core * half, half)
    theirs = pl.multiple_of((1 - core) * half, half)
    pairs = [
        (rates_ref, rates_out),
        (own_ref, lhs_out.at[:, pl.ds(mine, half)]),
        (other_ref, lhs_out.at[:, pl.ds(theirs, half)]),
        (filt_ref, filt_out),
        (w_ref.at[pl.ds(1, w_out.shape[0])], w_out),
    ]
    copies = [pltpu.make_async_copy(src, dst, sems.at[i]) for i, (src, dst) in enumerate(pairs)]
    for copy in copies:
        copy.start()
    copies[0].wait()
    rates = rates_out[...]
    rest, span, after = where_ref[0] // 2, rows, 0

    def decay(tokens):
        return jnp.exp(-rates * jnp.asarray(tokens, F32))

    for level in range(len(SEQ)):
        here = lax.rem(rest, RING)
        rest = rest // RING
        total_out[RING * level] = decay(span * (RING - 1 - here))
        for k in range(1, RING):
            inside = (k <= here).astype(F32)
            into_out[(RING - 1) * level + k - 1] = inside * decay(span * (k - 1) + after)
            place = lax.rem(here - k + RING, RING)
            total_out[RING * level + k] = decay(span * (RING - 1 - place))
        after = after + span * here
        span = span * RING
    for copy in copies[1:]:
        copy.wait()


def stage_call(where, own, other, weight, filt, rates):
    rows, half = own.shape
    vmem = pl.BlockSpec(memory_space=pltpu.VMEM)
    anywhere = pl.BlockSpec(memory_space=pl.ANY)
    inputs = [pltpu.with_memory_space_constraint(x, pltpu.HBM) for x in (own, weight, filt, rates)]
    return pl.pallas_call(
        stage_kernel,
        in_specs=[pl.BlockSpec(memory_space=pltpu.SMEM)] + [anywhere] * 5,
        out_specs=[vmem] * 6,
        out_shape=[
            pltpu.VMEM((rows, 2 * half), BF16),
            pltpu.VMEM((weight.shape[0] - 1, *weight.shape[1:]), BF16),
            pltpu.VMEM(filt.shape, F32),
            pltpu.VMEM(rates.shape, F32),
            pltpu.VMEM((len(SEQ) * (RING - 1), *rates.shape), F32),
            pltpu.VMEM((len(SEQ) * RING, *rates.shape), F32),
        ],
        scratch_shapes=[pltpu.SemaphoreType.DMA((5,))],
        compiler_params=pltpu.CompilerParams(vmem_limit_bytes=4 * MIB),
        name="stage",
    )(where, inputs[0], other, *inputs[1:])


def hold_segments(held, part, first, per):
    steps = held.shape[1] // SEGS - HISTORY
    pitch = steps + HISTORY
    for l in range(WIDTH // LANES):
        lanes = slice(l * LANES, (l + 1) * LANES)
        for g in range(first, first + per):
            row = (g - first) * steps + (0 if first else HALO)
            held[l, g * pitch + HISTORY : (g + 1) * pitch] = part[row : row + steps, lanes]
            if g == 0:
                held[l, :HISTORY] = part[row - HISTORY : row, lanes]
            if g + 1 < SEGS:
                held[l, (g + 1) * pitch : (g + 1) * pitch + HISTORY] = part[
                    row + steps - HISTORY : row + steps, lanes
                ]


def join_halo(where_ref, halo_ref, own_ref, other_ref):
    half = own_ref.shape[1]
    core = lax.rem(where_ref[0], 2)
    halo_ref[:, pl.ds(pl.multiple_of(core * half, half), half)] = own_ref[...]
    halo_ref[:, pl.ds(pl.multiple_of((1 - core) * half, half), half)] = other_ref[...]


def segment_rows(lhs_ref, halo_ref, first, per):
    steps = lhs_ref.shape[0] // SEGS
    rows = lhs_ref[first * steps : (first + per) * steps]
    return rows if first else jnp.concatenate([halo_ref[...], rows], axis=0)


def front_kernel(
    where_ref,
    lhs_ref,
    halo_own_ref,
    halo_other_ref,
    w_ref,
    wq_ref,
    filt_ref,
    rates_ref,
    source_ref,
    ends_ref,
    total_ref,
    staged_ref,
    halo_ref,
    proj_a,
    proj_b,
    sem,
):
    rows = lhs_ref.shape[0]
    steps = rows // SEGS
    pitch = steps + HISTORY
    modes = rates_ref.shape[0]
    streams = w_ref.shape[0]
    tiles = w_ref.shape[2] // WIDTH
    per = SEGS // 2
    proj = (proj_a, proj_b)

    stage = pltpu.make_async_copy(wq_ref.at[0], staged_ref, sem)
    stage.start()
    join_halo(where_ref, halo_ref, halo_own_ref, halo_other_ref)

    def projection(tile):
        held = proj[tile % 2]

        def piece(j, first):
            part = jnp.dot(
                segment_rows(lhs_ref, halo_ref, first, per),
                w_ref[j, :, tile * WIDTH : (tile + 1) * WIDTH],
                preferred_element_type=F32,
            )
            hold_segments(held.at[j], part, first, per)

        return [
            lambda j=j, first=first: piece(j, first)
            for j in range(streams)
            for first in range(0, SEGS, per)
        ]

    def recurrence(tile, size=4):
        held = proj[tile % 2]
        pieces = []
        for l in range(WIDTH // LANES):
            lanes = slice(tile * WIDTH + l * LANES, tile * WIDTH + (l + 1) * LANES)
            kept = {}

            def at(j, t, l=l):
                return held[j, l, pl.ds(HISTORY + t, SEGS, stride=pitch), :]

            def begin(kept=kept, lanes=lanes, at=at):
                kept["taps"] = [
                    [spread(filt_ref[a, j + 1 : j + 2, lanes]) for a in range(3)]
                    for j in range(streams)
                ]
                kept["decay"] = [spread(jnp.exp(-rates_ref[n : n + 1, lanes])) for n in range(modes)]
                kept["one"] = [at(j, -1) for j in range(streams)]
                kept["two"] = [at(j, -2) for j in range(streams)]
                kept["state"] = [jnp.zeros((SEGS, LANES), F32)] * modes

            def advance(t0, kept=kept, lanes=lanes, at=at):
                for t in range(t0, t0 + size):
                    now = [at(j, t) for j in range(streams)]
                    k, v = [
                        filtered_step(*terms)
                        for terms in zip(kept["taps"], now, kept["one"], kept["two"])
                    ]
                    kept["one"], kept["two"] = now, kept["one"]
                    source = k * v
                    kept["state"] = [d * s + source for d, s in zip(kept["decay"], kept["state"])]
                    source_ref[t * SEGS : (t + 1) * SEGS, lanes] = source

            def finish(kept=kept, lanes=lanes):
                seg = lax.broadcasted_iota(jnp.int32, (SEGS, LANES), 0)
                later = (SEGS - 1 - seg).astype(F32) * float(steps)
                for n, state in enumerate(kept["state"]):
                    ends_ref[n * SEGS : (n + 1) * SEGS, lanes] = state
                    weight = jnp.exp(-spread(rates_ref[n : n + 1, lanes]) * later)
                    total_ref[n : n + 1, lanes] = jnp.sum(state * weight, axis=0, keepdims=True)

            pieces += [begin]
            pieces += [lambda t0=t0, advance=advance: advance(t0) for t0 in range(0, steps, size)]
            pieces += [finish]
        return pieces

    for work in projection(0):
        work()
    for tile in range(tiles):
        slow = projection(tile + 1) if tile + 1 < tiles else [lambda: None]
        fast = recurrence(tile)
        done = 0
        for i, work in enumerate(slow):
            work()
            upto = (i + 1) * len(fast) // len(slow)
            for step in fast[done:upto]:
                step()
            done = upto
    stage.wait()


def front_call(where, lhs, halo_own, halo_other, staged, weight, filt, rates):
    rows, full = lhs.shape
    streams, _, channels = staged.shape
    modes = rates.shape[0]
    vmem = pl.BlockSpec(memory_space=pltpu.VMEM)
    held = pltpu.VMEM((streams, WIDTH // LANES, rows + SEGS * HISTORY, LANES), F32)
    return pl.pallas_call(
        front_kernel,
        in_specs=[pl.BlockSpec(memory_space=pltpu.SMEM)]
        + [vmem] * 4
        + [pl.BlockSpec(memory_space=pl.ANY)]
        + [vmem] * 2,
        out_specs=[vmem] * 4,
        out_shape=[
            pltpu.VMEM((rows, channels), F32),
            pltpu.VMEM((modes * SEGS, channels), F32),
            pltpu.VMEM((modes, channels), F32),
            pltpu.VMEM((full, channels), BF16),
        ],
        scratch_shapes=[pltpu.VMEM((HALO, full), BF16), held, held, pltpu.SemaphoreType.DMA],
        compiler_params=pltpu.CompilerParams(vmem_limit_bytes=10 * MIB),
        name="front",
    )(
        where,
        lhs,
        halo_own,
        halo_other,
        staged,
        pltpu.with_memory_space_constraint(weight, pltpu.HBM),
        filt,
        rates,
    )


def query_kernel(where_ref, lhs_ref, halo_own_ref, halo_other_ref, w_ref, filt_ref, query_ref, halo_ref, held):
    steps = lhs_ref.shape[0] // SEGS
    pitch = steps + HISTORY
    per = SEGS // 2
    join_halo(where_ref, halo_ref, halo_own_ref, halo_other_ref)
    for tile in range(w_ref.shape[1] // WIDTH):
        for first in range(0, SEGS, per):
            part = jnp.dot(
                segment_rows(lhs_ref, halo_ref, first, per),
                w_ref[:, tile * WIDTH : (tile + 1) * WIDTH],
                preferred_element_type=F32,
            )
            hold_segments(held.at[tile], part, first, per)
        for l in range(WIDTH // LANES):
            lanes = slice(tile * WIDTH + l * LANES, tile * WIDTH + (l + 1) * LANES)
            taps = [spread(filt_ref[a, 0:1, lanes]) for a in range(3)]

            def at(t, tile=tile, l=l):
                return held[tile, l, pl.ds(HISTORY + t, SEGS, stride=pitch), :]

            one, two = at(-1), at(-2)
            for t in range(steps):
                now = at(t)
                query_ref[t * SEGS : (t + 1) * SEGS, lanes] = filtered_step(taps, now, one, two)
                one, two = now, one


def query_call(where, lhs, halo_own, halo_other, weight, filt):
    rows, full = lhs.shape
    channels = weight.shape[1]
    vmem = pl.BlockSpec(memory_space=pltpu.VMEM)
    args = [
        pltpu.with_memory_space_constraint(x, pltpu.VMEM)
        for x in (lhs, halo_own, halo_other, weight, filt)
    ]
    return pl.pallas_call(
        query_kernel,
        in_specs=[pl.BlockSpec(memory_space=pltpu.SMEM)] + [vmem] * 5,
        out_specs=vmem,
        out_shape=pltpu.VMEM((rows, channels), F32),
        scratch_shapes=[
            pltpu.VMEM((HALO, full), BF16),
            pltpu.VMEM((channels // WIDTH, WIDTH // LANES, rows + SEGS * HISTORY, LANES), F32),
        ],
        compiler_params=pltpu.CompilerParams(vmem_limit_bytes=6 * MIB),
        cost_estimate=pl.CostEstimate(
            flops=2 * (rows + HALO) * full * channels, transcendentals=0, bytes_accessed=0
        ),
        name="query",
    )(where, *args)


def local_kernel(first, source_ref, rates_ref, gain_ref, local_ref):
    rows, channels = local_ref.shape
    modes = rates_ref.shape[0]
    for i in range(channels // LANES):
        lanes = slice(first + i * LANES, first + (i + 1) * LANES)
        decays = [spread(jnp.exp(-rates_ref[n : n + 1, lanes])) for n in range(modes)]
        gains = [spread(gain_ref[n : n + 1, lanes]) for n in range(modes)]

        def body(t, states, i=i, lanes=lanes, decays=decays, gains=gains):
            row = pl.ds(pl.multiple_of(t * SEGS, SEGS), SEGS)
            source = source_ref[row, lanes]
            states = tuple(d * s + source for d, s in zip(decays, states))
            local_ref[row, i * LANES : (i + 1) * LANES] = tree_sum(
                [g * s for g, s in zip(gains, states)]
            )
            return states

        zero = jnp.zeros((SEGS, LANES), F32)
        lax.fori_loop(0, rows // SEGS, body, (zero,) * modes, unroll=16)


def local_call(source, rates, gain, part):
    rows, channels = source.shape
    vmem = pl.BlockSpec(memory_space=pltpu.VMEM)
    args = [pltpu.with_memory_space_constraint(x, pltpu.VMEM) for x in (source, rates, gain)]
    return pl.pallas_call(
        functools.partial(local_kernel, part * channels // PARTS),
        in_specs=[vmem] * 3,
        out_specs=vmem,
        out_shape=pltpu.VMEM((rows, channels // PARTS), F32),
        compiler_params=pltpu.CompilerParams(vmem_limit_bytes=4 * MIB),
        cost_estimate=pl.CostEstimate(
            flops=4 * rates.shape[0] * rows * channels // PARTS, transcendentals=0, bytes_accessed=0
        ),
        name="local",
    )(*args)


def hidden_kernel(ends_ref, into_ref, first_ref, second_ref, query_ref, rates_ref, gain_ref, hidden_ref):
    rows, channels = query_ref.shape
    steps = rows // SEGS
    modes = rates_ref.shape[0]
    local_refs = (first_ref, second_ref)
    seg = lax.broadcasted_iota(jnp.int32, (SEGS, LANES), 0)
    for i in range(channels // LANES):
        lanes = slice(i * LANES, (i + 1) * LANES)
        local_ref = local_refs[i * LANES * PARTS // channels]
        here = slice(lanes.start % (channels // PARTS), lanes.start % (channels // PARTS) + LANES)
        decays, leads = [], []
        for n in range(modes):
            rate = spread(rates_ref[n : n + 1, lanes])
            state = pltpu.roll(ends_ref[n * SEGS : (n + 1) * SEGS, lanes], 1, 0)
            state = jnp.where(seg == 0, spread(into_ref[n : n + 1, lanes]), state)
            for hop in (1, 2, 4):
                earlier = pltpu.roll(state, hop, 0) * jnp.exp(-rate * float(steps * hop))
                state = state + jnp.where(seg >= hop, earlier, 0.0)
            decays.append(jnp.exp(-rate))
            leads.append(spread(gain_ref[n : n + 1, lanes]) * state)

        def body(t, leads, lanes=lanes, here=here, local_ref=local_ref, decays=decays):
            halves = []
            for u in range(2):
                row = pl.ds(pl.multiple_of((2 * t + u) * SEGS, SEGS), SEGS)
                leads = tuple(d * s for d, s in zip(decays, leads))
                halves.append(query_ref[row, lanes] * (local_ref[row, here] + tree_sum(leads)))
            row = pl.ds(pl.multiple_of(2 * t * SEGS, 2 * SEGS), 2 * SEGS)
            hidden_ref[row, lanes] = jnp.concatenate(halves, axis=0).astype(BF16)
            return leads

        lax.fori_loop(0, steps // 2, body, tuple(leads), unroll=8)


def hidden_call(ends, into, local, query, rates, gain):
    vmem = pl.BlockSpec(memory_space=pltpu.VMEM)
    args = [
        pltpu.with_memory_space_constraint(x, pltpu.VMEM)
        for x in (ends, into, *local, query, rates, gain)
    ]
    return pl.pallas_call(
        hidden_kernel,
        in_specs=[vmem] * 7,
        out_specs=vmem,
        out_shape=pltpu.VMEM(query.shape, BF16),
        compiler_params=pltpu.CompilerParams(vmem_limit_bytes=4 * MIB),
        name="hidden",
    )(*args)


def product_kernel(where_ref, hidden_ref, w_ref, w_other_ref, part_ref, staged_ref, mine_ref, sems):
    columns = part_ref.shape[1]
    lanes = pl.ds(pl.multiple_of(lax.rem(where_ref[0], 2) * columns, columns), columns)
    mine = pltpu.make_async_copy(w_ref.at[:, lanes], mine_ref, sems.at[0])
    theirs = pltpu.make_async_copy(w_other_ref.at[:, lanes], staged_ref, sems.at[1])
    mine.start()
    theirs.start()
    mine.wait()
    part_ref[...] = jnp.dot(hidden_ref[...], mine_ref[...], preferred_element_type=F32)
    theirs.wait()


def product_call(where, hidden, weight, weight_other):
    rows, channels = hidden.shape
    columns = weight.shape[1] // 2
    vmem = pl.BlockSpec(memory_space=pltpu.VMEM)
    anywhere = pl.BlockSpec(memory_space=pl.ANY)
    return pl.pallas_call(
        product_kernel,
        in_specs=[pl.BlockSpec(memory_space=pltpu.SMEM), vmem, anywhere, anywhere],
        out_specs=[vmem] * 2,
        out_shape=[pltpu.VMEM((rows, columns), F32), pltpu.VMEM((channels, columns), BF16)],
        scratch_shapes=[pltpu.VMEM((channels, columns), BF16), pltpu.SemaphoreType.DMA((2,))],
        compiler_params=pltpu.CompilerParams(vmem_limit_bytes=8 * MIB),
        name="product",
    )(where, hidden, weight, weight_other)


def output_kernel(part_ref, other_ref, w_ref, out_ref, acc_ref, rows_ref, sems):
    rows, columns = part_ref.shape
    steps = rows // SEGS
    copies = []
    for tile in range(columns // WIDTH):
        lanes = slice(tile * WIDTH, (tile + 1) * WIDTH)
        part = part_ref[:, lanes] + jnp.dot(
            other_ref[...], w_ref[:, lanes], preferred_element_type=F32
        )
        for l in range(WIDTH // LANES):
            acc_ref[tile, l] = part[:, l * LANES : (l + 1) * LANES]
            for j in range(SEGS):
                rows_ref[
                    j * steps : (j + 1) * steps,
                    tile * WIDTH + l * LANES : tile * WIDTH + (l + 1) * LANES,
                ] = acc_ref[tile, l, pl.ds(j, steps, stride=SEGS), :]
        copies.append(pltpu.make_async_copy(rows_ref.at[:, lanes], out_ref.at[:, lanes], sems.at[tile]))
        copies[-1].start()
    for copy in copies:
        copy.wait()


def output_call(part, other, weight):
    rows, columns = part.shape
    vmem = pl.BlockSpec(memory_space=pltpu.VMEM)
    args = [pltpu.with_memory_space_constraint(x, pltpu.VMEM) for x in (part, other, weight)]
    return pl.pallas_call(
        output_kernel,
        in_specs=[vmem] * 3,
        out_specs=pl.BlockSpec(memory_space=pl.ANY),
        out_shape=jax.ShapeDtypeStruct((rows, columns), F32),
        scratch_shapes=[
            pltpu.VMEM((columns // WIDTH, WIDTH // LANES, rows, LANES), F32),
            pltpu.VMEM((rows, columns), F32),
            pltpu.SemaphoreType.DMA((columns // WIDTH,)),
        ],
        compiler_params=pltpu.CompilerParams(vmem_limit_bytes=8 * MIB),
        name="output",
    )(*args)


def swapped(x):
    return lax.ppermute(x, "ch", [(0, 1), (1, 0)])


def from_before(x):
    count = RING**3
    return lax.ppermute(x, SEQ, [(i, i + 1) for i in range(count - 1)])


def round_the_ring(state, axis):
    sent = state.astype(BF16)
    return [
        lax.ppermute(sent, axis, [(i, (i + k) % RING) for i in range(RING)])
        for k in range(1, RING)
    ]


def on_device(tokens, in_weight, short_filter, residues, rates, out_weight):
    rows = tokens.shape[0]
    where = lax.axis_index((*SEQ, "ch")).astype(jnp.int32).reshape(1)
    weight = in_weight.transpose(1, 0, 2)
    rates = rates.T
    gain = residues.T * jnp.sqrt(1.0 - jnp.exp(-2.0 * rates))

    halo_own = from_before(tokens[rows - HALO :])
    lhs, staged, filt, rates, into_weights, total_weights = stage_call(
        where, tokens, swapped(tokens), weight, short_filter, rates
    )
    halo_own, lhs, out_weight = lax.optimization_barrier((halo_own, lhs, out_weight))
    halo_other = swapped(halo_own)
    lhs, halo_other, out_weight = lax.optimization_barrier((lhs, halo_other, out_weight))
    out_weight_other = swapped(out_weight)
    source, ends, total, query_weight = front_call(
        where, lhs, halo_own, halo_other, staged, weight, filt, rates
    )
    beside = [
        query_call(where, lhs, halo_own, halo_other, query_weight, filt),
        *[local_call(source, rates, gain, part) for part in range(PARTS)],
    ]

    into = 0.0
    for level, axis in enumerate(reversed(SEQ)):
        arrived = round_the_ring(total, axis)
        beside[level], *arrived = lax.optimization_barrier((beside[level], *arrived))
        total = total_weights[RING * level] * total
        for k, part in enumerate(arrived):
            part = part.astype(F32)
            into = into + into_weights[(RING - 1) * level + k] * part
            total = total + total_weights[RING * level + k + 1] * part

    hidden = hidden_call(ends, into, beside[1:], beside[0], rates, gain)
    part, partner_weight = product_call(where, hidden, out_weight, out_weight_other)
    return output_call(part, swapped(hidden), partner_weight)


def solution(mesh):
    cube = Mesh(mesh.devices.reshape(RING, RING, RING, 2), (*SEQ, "ch"))
    return jax.shard_map(
        on_device,
        mesh=cube,
        in_specs=(
            P(SEQ, "ch"),
            P(None, None, "ch"),
            P(None, None, "ch"),
            P("ch", None),
            P("ch", None),
            P("ch", None),
        ),
        out_specs=P(SEQ, "ch"),
        check_vma=False,
    )
```

```python
import functools

import jax
import jax.numpy as jnp
from jax import lax
from jax.experimental import pallas as pl
from jax.experimental.pallas import tpu as pltpu
from jax.sharding import Mesh, PartitionSpec as P

SEGS = 8
HALO = 16
LANES = 128
HISTORY = 8
WIDTH = 256
AHEAD = 2
SEQ = ("z", "y", "x")
RING = 4
PARTS = 2
F32 = jnp.float32
BF16 = jnp.bfloat16
MIB = 1024 * 1024


def spread(row):
    return jnp.broadcast_to(row, (SEGS, row.shape[-1]))


def filtered_step(taps, now, one, two):
    return taps[0] * now + taps[1] * one + taps[2] * two


def tree_sum(parts):
    parts = list(parts)
    while len(parts) > 1:
        parts = [a + b for a, b in zip(parts[::2], parts[1::2])]
    return parts[0]


def stage_kernel(
    where_ref,
    own_ref,
    other_ref,
    w_ref,
    filt_ref,
    rates_ref,
    lhs_out,
    w_out,
    filt_out,
    rates_out,
    into_out,
    total_out,
    sems,
):
    rows, half = own_ref.shape
    core = lax.rem(where_ref[0], 2)
    mine = pl.multiple_of(core * half, half)
    theirs = pl.multiple_of((1 - core) * half, half)
    pairs = [
        (rates_ref, rates_out),
        (own_ref, lhs_out.at[:, pl.ds(mine, half)]),
        (other_ref, lhs_out.at[:, pl.ds(theirs, half)]),
        (filt_ref, filt_out),
        (w_ref.at[pl.ds(1, w_out.shape[0]), :, pl.ds(0, w_out.shape[2])], w_out),
    ]
    copies = [pltpu.make_async_copy(src, dst, sems.at[i]) for i, (src, dst) in enumerate(pairs)]
    for copy in copies:
        copy.start()
    copies[0].wait()
    rates = rates_out[...]
    rest, span, after = where_ref[0] // 2, rows, 0

    def decay(tokens):
        return jnp.exp(-rates * jnp.asarray(tokens, F32))

    for level in range(len(SEQ)):
        here = lax.rem(rest, RING)
        rest = rest // RING
        total_out[RING * level] = decay(span * (RING - 1 - here))
        for k in range(1, RING):
            inside = (k <= here).astype(F32)
            into_out[(RING - 1) * level + k - 1] = inside * decay(span * (k - 1) + after)
            place = lax.rem(here - k + RING, RING)
            total_out[RING * level + k] = decay(span * (RING - 1 - place))
        after = after + span * here
        span = span * RING
    for copy in copies[1:]:
        copy.wait()


def stage_call(where, own, other, weight, filt, rates):
    rows, half = own.shape
    vmem = pl.BlockSpec(memory_space=pltpu.VMEM)
    anywhere = pl.BlockSpec(memory_space=pl.ANY)
    inputs = [pltpu.with_memory_space_constraint(x, pltpu.HBM) for x in (own, weight, filt, rates)]
    return pl.pallas_call(
        stage_kernel,
        in_specs=[pl.BlockSpec(memory_space=pltpu.SMEM)] + [anywhere] * 5,
        out_specs=[vmem] * 6,
        out_shape=[
            pltpu.VMEM((rows, 2 * half), BF16),
            pltpu.VMEM((weight.shape[0] - 1, weight.shape[1], AHEAD * WIDTH), BF16),
            pltpu.VMEM(filt.shape, F32),
            pltpu.VMEM(rates.shape, F32),
            pltpu.VMEM((len(SEQ) * (RING - 1), *rates.shape), F32),
            pltpu.VMEM((len(SEQ) * RING, *rates.shape), F32),
        ],
        scratch_shapes=[pltpu.SemaphoreType.DMA((5,))],
        compiler_params=pltpu.CompilerParams(vmem_limit_bytes=4 * MIB),
        name="stage",
    )(where, inputs[0], other, *inputs[1:])


def hold_segments(held, part, first, per):
    steps = held.shape[1] // SEGS - HISTORY
    pitch = steps + HISTORY
    for l in range(WIDTH // LANES):
        lanes = slice(l * LANES, (l + 1) * LANES)
        for g in range(first, first + per):
            row = (g - first) * steps + (0 if first else HALO)
            held[l, g * pitch + HISTORY : (g + 1) * pitch] = part[row : row + steps, lanes]
            if g == 0:
                held[l, :HISTORY] = part[row - HISTORY : row, lanes]
            if g + 1 < SEGS:
                held[l, (g + 1) * pitch : (g + 1) * pitch + HISTORY] = part[
                    row + steps - HISTORY : row + steps, lanes
                ]


def join_halo(where_ref, halo_ref, own_ref, other_ref):
    half = own_ref.shape[1]
    core = lax.rem(where_ref[0], 2)
    halo_ref[:, pl.ds(pl.multiple_of(core * half, half), half)] = own_ref[...]
    halo_ref[:, pl.ds(pl.multiple_of((1 - core) * half, half), half)] = other_ref[...]


def segment_rows(lhs_ref, halo_ref, first, per):
    steps = lhs_ref.shape[0] // SEGS
    rows = lhs_ref[first * steps : (first + per) * steps]
    return rows if first else jnp.concatenate([halo_ref[...], rows], axis=0)


def front_kernel(
    where_ref,
    lhs_ref,
    halo_own_ref,
    halo_other_ref,
    ahead_ref,
    w_ref,
    filt_ref,
    rates_ref,
    source_ref,
    ends_ref,
    total_ref,
    staged_ref,
    halo_ref,
    rest_ref,
    proj_a,
    proj_b,
    sems,
):
    rows = lhs_ref.shape[0]
    steps = rows // SEGS
    pitch = steps + HISTORY
    modes = rates_ref.shape[0]
    streams = ahead_ref.shape[0]
    tiles = w_ref.shape[2] // WIDTH
    per = SEGS // 2
    proj = (proj_a, proj_b)

    rest = pltpu.make_async_copy(
        w_ref.at[pl.ds(1, streams), :, pl.ds(AHEAD * WIDTH, (tiles - AHEAD) * WIDTH)],
        rest_ref,
        sems.at[0],
    )
    stage = pltpu.make_async_copy(w_ref.at[0], staged_ref, sems.at[1])
    rest.start()
    stage.start()
    join_halo(where_ref, halo_ref, halo_own_ref, halo_other_ref)

    def projection(tile):
        held = proj[tile % 2]
        weights, column = (ahead_ref, tile) if tile < AHEAD else (rest_ref, tile - AHEAD)
        if tile == AHEAD:
            rest.wait()

        def piece(j, first):
            part = jnp.dot(
                segment_rows(lhs_ref, halo_ref, first, per),
                weights[j, :, column * WIDTH : (column + 1) * WIDTH],
                preferred_element_type=F32,
            )
            hold_segments(held.at[j], part, first, per)

        return [
            lambda j=j, first=first: piece(j, first)
            for j in range(streams)
            for first in range(0, SEGS, per)
        ]

    def recurrence(tile, size=4):
        held = proj[tile % 2]
        pieces = []
        for l in range(WIDTH // LANES):
            lanes = slice(tile * WIDTH + l * LANES, tile * WIDTH + (l + 1) * LANES)
            kept = {}

            def at(j, t, l=l):
                return held[j, l, pl.ds(HISTORY + t, SEGS, stride=pitch), :]

            def begin(kept=kept, lanes=lanes, at=at):
                kept["taps"] = [
                    [spread(filt_ref[a, j + 1 : j + 2, lanes]) for a in range(3)]
                    for j in range(streams)
                ]
                kept["decay"] = [spread(jnp.exp(-rates_ref[n : n + 1, lanes])) for n in range(modes)]
                kept["one"] = [at(j, -1) for j in range(streams)]
                kept["two"] = [at(j, -2) for j in range(streams)]
                kept["state"] = [jnp.zeros((SEGS, LANES), F32)] * modes

            def advance(t0, kept=kept, lanes=lanes, at=at):
                for t in range(t0, t0 + size):
                    now = [at(j, t) for j in range(streams)]
                    k, v = [
                        filtered_step(*terms)
                        for terms in zip(kept["taps"], now, kept["one"], kept["two"])
                    ]
                    kept["one"], kept["two"] = now, kept["one"]
                    source = k * v
                    kept["state"] = [d * s + source for d, s in zip(kept["decay"], kept["state"])]
                    source_ref[t * SEGS : (t + 1) * SEGS, lanes] = source

            def finish(kept=kept, lanes=lanes):
                seg = lax.broadcasted_iota(jnp.int32, (SEGS, LANES), 0)
                later = (SEGS - 1 - seg).astype(F32) * float(steps)
                for n, state in enumerate(kept["state"]):
                    ends_ref[n * SEGS : (n + 1) * SEGS, lanes] = state
                    weight = jnp.exp(-spread(rates_ref[n : n + 1, lanes]) * later)
                    total_ref[n : n + 1, lanes] = jnp.sum(state * weight, axis=0, keepdims=True)

            pieces += [begin]
            pieces += [lambda t0=t0, advance=advance: advance(t0) for t0 in range(0, steps, size)]
            pieces += [finish]
        return pieces

    for work in projection(0):
        work()
    for tile in range(tiles):
        slow = projection(tile + 1) if tile + 1 < tiles else [lambda: None]
        fast = recurrence(tile)
        done = 0
        for i, work in enumerate(slow):
            work()
            upto = (i + 1) * len(fast) // len(slow)
            for step in fast[done:upto]:
                step()
            done = upto
    stage.wait()


def front_call(where, lhs, halo_own, halo_other, ahead, weight, filt, rates):
    rows, full = lhs.shape
    streams, channels = ahead.shape[0], weight.shape[2]
    modes = rates.shape[0]
    vmem = pl.BlockSpec(memory_space=pltpu.VMEM)
    held = pltpu.VMEM((streams, WIDTH // LANES, rows + SEGS * HISTORY, LANES), F32)
    return pl.pallas_call(
        front_kernel,
        in_specs=[pl.BlockSpec(memory_space=pltpu.SMEM)]
        + [vmem] * 4
        + [pl.BlockSpec(memory_space=pl.ANY)]
        + [vmem] * 2,
        out_specs=[vmem] * 4,
        out_shape=[
            pltpu.VMEM((rows, channels), F32),
            pltpu.VMEM((modes * SEGS, channels), F32),
            pltpu.VMEM((modes, channels), F32),
            pltpu.VMEM((full, channels), BF16),
        ],
        scratch_shapes=[
            pltpu.VMEM((HALO, full), BF16),
            pltpu.VMEM((streams, full, channels - AHEAD * WIDTH), BF16),
            held,
            held,
            pltpu.SemaphoreType.DMA((2,)),
        ],
        compiler_params=pltpu.CompilerParams(vmem_limit_bytes=14 * MIB),
        name="front",
    )(
        where,
        lhs,
        halo_own,
        halo_other,
        ahead,
        pltpu.with_memory_space_constraint(weight, pltpu.HBM),
        filt,
        rates,
    )


def query_kernel(where_ref, lhs_ref, halo_own_ref, halo_other_ref, w_ref, filt_ref, query_ref, halo_ref, held):
    steps = lhs_ref.shape[0] // SEGS
    pitch = steps + HISTORY
    per = SEGS // 2
    join_halo(where_ref, halo_ref, halo_own_ref, halo_other_ref)
    for tile in range(w_ref.shape[1] // WIDTH):
        for first in range(0, SEGS, per):
            part = jnp.dot(
                segment_rows(lhs_ref, halo_ref, first, per),
                w_ref[:, tile * WIDTH : (tile + 1) * WIDTH],
                preferred_element_type=F32,
            )
            hold_segments(held.at[tile], part, first, per)
        for l in range(WIDTH // LANES):
            lanes = slice(tile * WIDTH + l * LANES, tile * WIDTH + (l + 1) * LANES)
            taps = [spread(filt_ref[a, 0:1, lanes]) for a in range(3)]

            def at(t, tile=tile, l=l):
                return held[tile, l, pl.ds(HISTORY + t, SEGS, stride=pitch), :]

            one, two = at(-1), at(-2)
            for t in range(steps):
                now = at(t)
                query_ref[t * SEGS : (t + 1) * SEGS, lanes] = filtered_step(taps, now, one, two)
                one, two = now, one


def query_call(where, lhs, halo_own, halo_other, weight, filt):
    rows, full = lhs.shape
    channels = weight.shape[1]
    vmem = pl.BlockSpec(memory_space=pltpu.VMEM)
    args = [
        pltpu.with_memory_space_constraint(x, pltpu.VMEM)
        for x in (lhs, halo_own, halo_other, weight, filt)
    ]
    return pl.pallas_call(
        query_kernel,
        in_specs=[pl.BlockSpec(memory_space=pltpu.SMEM)] + [vmem] * 5,
        out_specs=vmem,
        out_shape=pltpu.VMEM((rows, channels), F32),
        scratch_shapes=[
            pltpu.VMEM((HALO, full), BF16),
            pltpu.VMEM((channels // WIDTH, WIDTH // LANES, rows + SEGS * HISTORY, LANES), F32),
        ],
        compiler_params=pltpu.CompilerParams(vmem_limit_bytes=6 * MIB),
        cost_estimate=pl.CostEstimate(
            flops=2 * (rows + HALO) * full * channels, transcendentals=0, bytes_accessed=0
        ),
        name="query",
    )(where, *args)


def local_kernel(first, source_ref, rates_ref, gain_ref, local_ref):
    rows, channels = local_ref.shape
    modes = rates_ref.shape[0]
    for i in range(channels // LANES):
        lanes = slice(first + i * LANES, first + (i + 1) * LANES)
        decays = [spread(jnp.exp(-rates_ref[n : n + 1, lanes])) for n in range(modes)]
        gains = [spread(gain_ref[n : n + 1, lanes]) for n in range(modes)]

        def body(t, states, i=i, lanes=lanes, decays=decays, gains=gains):
            row = pl.ds(pl.multiple_of(t * SEGS, SEGS), SEGS)
            source = source_ref[row, lanes]
            states = tuple(d * s + source for d, s in zip(decays, states))
            local_ref[row, i * LANES : (i + 1) * LANES] = tree_sum(
                [g * s for g, s in zip(gains, states)]
            )
            return states

        zero = jnp.zeros((SEGS, LANES), F32)
        lax.fori_loop(0, rows // SEGS, body, (zero,) * modes, unroll=16)


def local_call(source, rates, gain, part):
    rows, channels = source.shape
    vmem = pl.BlockSpec(memory_space=pltpu.VMEM)
    args = [pltpu.with_memory_space_constraint(x, pltpu.VMEM) for x in (source, rates, gain)]
    return pl.pallas_call(
        functools.partial(local_kernel, part * channels // PARTS),
        in_specs=[vmem] * 3,
        out_specs=vmem,
        out_shape=pltpu.VMEM((rows, channels // PARTS), F32),
        compiler_params=pltpu.CompilerParams(vmem_limit_bytes=4 * MIB),
        cost_estimate=pl.CostEstimate(
            flops=4 * rates.shape[0] * rows * channels // PARTS, transcendentals=0, bytes_accessed=0
        ),
        name="local",
    )(*args)


def hidden_kernel(ends_ref, into_ref, first_ref, second_ref, query_ref, rates_ref, gain_ref, hidden_ref):
    rows, channels = query_ref.shape
    steps = rows // SEGS
    modes = rates_ref.shape[0]
    local_refs = (first_ref, second_ref)
    seg = lax.broadcasted_iota(jnp.int32, (SEGS, LANES), 0)
    for i in range(channels // LANES):
        lanes = slice(i * LANES, (i + 1) * LANES)
        local_ref = local_refs[i * LANES * PARTS // channels]
        here = slice(lanes.start % (channels // PARTS), lanes.start % (channels // PARTS) + LANES)
        decays, leads = [], []
        for n in range(modes):
            rate = spread(rates_ref[n : n + 1, lanes])
            state = pltpu.roll(ends_ref[n * SEGS : (n + 1) * SEGS, lanes], 1, 0)
            state = jnp.where(seg == 0, spread(into_ref[n : n + 1, lanes]), state)
            for hop in (1, 2, 4):
                earlier = pltpu.roll(state, hop, 0) * jnp.exp(-rate * float(steps * hop))
                state = state + jnp.where(seg >= hop, earlier, 0.0)
            decays.append(jnp.exp(-rate))
            leads.append(spread(gain_ref[n : n + 1, lanes]) * state)

        def body(t, leads, lanes=lanes, here=here, local_ref=local_ref, decays=decays):
            halves = []
            for u in range(2):
                row = pl.ds(pl.multiple_of((2 * t + u) * SEGS, SEGS), SEGS)
                leads = tuple(d * s for d, s in zip(decays, leads))
                halves.append(query_ref[row, lanes] * (local_ref[row, here] + tree_sum(leads)))
            row = pl.ds(pl.multiple_of(2 * t * SEGS, 2 * SEGS), 2 * SEGS)
            hidden_ref[row, lanes] = jnp.concatenate(halves, axis=0).astype(BF16)
            return leads

        lax.fori_loop(0, steps // 2, body, tuple(leads), unroll=True)


def hidden_call(ends, into, local, query, rates, gain):
    vmem = pl.BlockSpec(memory_space=pltpu.VMEM)
    args = [
        pltpu.with_memory_space_constraint(x, pltpu.VMEM)
        for x in (ends, into, *local, query, rates, gain)
    ]
    return pl.pallas_call(
        hidden_kernel,
        in_specs=[vmem] * 7,
        out_specs=vmem,
        out_shape=pltpu.VMEM(query.shape, BF16),
        compiler_params=pltpu.CompilerParams(vmem_limit_bytes=4 * MIB),
        name="hidden",
    )(*args)


def product_kernel(where_ref, hidden_ref, w_ref, w_other_ref, part_ref, staged_ref, mine_ref, sems):
    columns = part_ref.shape[1]
    lanes = pl.ds(pl.multiple_of(lax.rem(where_ref[0], 2) * columns, columns), columns)
    mine = pltpu.make_async_copy(w_ref.at[:, lanes], mine_ref, sems.at[0])
    theirs = pltpu.make_async_copy(w_other_ref.at[:, lanes], staged_ref, sems.at[1])
    mine.start()
    theirs.start()
    mine.wait()
    part_ref[...] = jnp.dot(hidden_ref[...], mine_ref[...], preferred_element_type=F32)
    theirs.wait()


def product_call(where, hidden, weight, weight_other):
    rows, channels = hidden.shape
    columns = weight.shape[1] // 2
    vmem = pl.BlockSpec(memory_space=pltpu.VMEM)
    anywhere = pl.BlockSpec(memory_space=pl.ANY)
    return pl.pallas_call(
        product_kernel,
        in_specs=[pl.BlockSpec(memory_space=pltpu.SMEM), vmem, anywhere, anywhere],
        out_specs=[vmem] * 2,
        out_shape=[pltpu.VMEM((rows, columns), F32), pltpu.VMEM((channels, columns), BF16)],
        scratch_shapes=[pltpu.VMEM((channels, columns), BF16), pltpu.SemaphoreType.DMA((2,))],
        compiler_params=pltpu.CompilerParams(vmem_limit_bytes=8 * MIB),
        name="product",
    )(where, hidden, weight, weight_other)


def output_kernel(part_ref, other_ref, w_ref, out_ref, acc_ref, rows_ref, sems):
    rows, columns = part_ref.shape
    steps = rows // SEGS
    copies = []
    for tile in range(columns // WIDTH):
        lanes = slice(tile * WIDTH, (tile + 1) * WIDTH)
        part = part_ref[:, lanes] + jnp.dot(
            other_ref[...], w_ref[:, lanes], preferred_element_type=F32
        )
        for l in range(WIDTH // LANES):
            acc_ref[tile, l] = part[:, l * LANES : (l + 1) * LANES]
            for j in range(SEGS):
                rows_ref[
                    j * steps : (j + 1) * steps,
                    tile * WIDTH + l * LANES : tile * WIDTH + (l + 1) * LANES,
                ] = acc_ref[tile, l, pl.ds(j, steps, stride=SEGS), :]
        copies.append(pltpu.make_async_copy(rows_ref.at[:, lanes], out_ref.at[:, lanes], sems.at[tile]))
        copies[-1].start()
    for copy in copies:
        copy.wait()


def output_call(part, other, weight):
    rows, columns = part.shape
    vmem = pl.BlockSpec(memory_space=pltpu.VMEM)
    args = [pltpu.with_memory_space_constraint(x, pltpu.VMEM) for x in (part, other, weight)]
    return pl.pallas_call(
        output_kernel,
        in_specs=[vmem] * 3,
        out_specs=pl.BlockSpec(memory_space=pl.ANY),
        out_shape=jax.ShapeDtypeStruct((rows, columns), F32),
        scratch_shapes=[
            pltpu.VMEM((columns // WIDTH, WIDTH // LANES, rows, LANES), F32),
            pltpu.VMEM((rows, columns), F32),
            pltpu.SemaphoreType.DMA((columns // WIDTH,)),
        ],
        compiler_params=pltpu.CompilerParams(vmem_limit_bytes=8 * MIB),
        name="output",
    )(*args)


def swapped(x):
    return lax.ppermute(x, "ch", [(0, 1), (1, 0)])


def from_before(x):
    count = RING**3
    return lax.ppermute(x, SEQ, [(i, i + 1) for i in range(count - 1)])


def round_the_ring(state, axis):
    sent = state.astype(BF16)
    return [
        lax.ppermute(sent, axis, [(i, (i + k) % RING) for i in range(RING)])
        for k in range(1, RING)
    ]


def on_device(tokens, in_weight, short_filter, residues, rates, out_weight):
    rows = tokens.shape[0]
    where = lax.axis_index((*SEQ, "ch")).astype(jnp.int32).reshape(1)
    weight = in_weight.transpose(1, 0, 2)
    rates = rates.T
    gain = residues.T * jnp.sqrt(1.0 - jnp.exp(-2.0 * rates))

    halo_own = from_before(tokens[rows - HALO :])
    lhs, ahead, filt, rates, into_weights, total_weights = stage_call(
        where, tokens, swapped(tokens), weight, short_filter, rates
    )
    halo_own, lhs, out_weight = lax.optimization_barrier((halo_own, lhs, out_weight))
    halo_other = swapped(halo_own)
    lhs, halo_other, out_weight = lax.optimization_barrier((lhs, halo_other, out_weight))
    out_weight_other = swapped(out_weight)
    source, ends, total, query_weight = front_call(
        where, lhs, halo_own, halo_other, ahead, weight, filt, rates
    )
    beside = [
        query_call(where, lhs, halo_own, halo_other, query_weight, filt),
        *[local_call(source, rates, gain, part) for part in range(PARTS)],
    ]

    into = 0.0
    for level, axis in enumerate(reversed(SEQ)):
        arrived = round_the_ring(total, axis)
        beside[level], *arrived = lax.optimization_barrier((beside[level], *arrived))
        total = total_weights[RING * level] * total
        for k, part in enumerate(arrived):
            part = part.astype(F32)
            into = into + into_weights[(RING - 1) * level + k] * part
            total = total + total_weights[RING * level + k + 1] * part

    hidden = hidden_call(ends, into, beside[1:], beside[0], rates, gain)
    part, partner_weight = product_call(where, hidden, out_weight, out_weight_other)
    return output_call(part, swapped(hidden), partner_weight)


def solution(mesh):
    cube = Mesh(mesh.devices.reshape(RING, RING, RING, 2), (*SEQ, "ch"))
    return jax.shard_map(
        on_device,
        mesh=cube,
        in_specs=(
            P(SEQ, "ch"),
            P(None, None, "ch"),
            P(None, None, "ch"),
            P("ch", None),
            P("ch", None),
            P("ch", None),
        ),
        out_specs=P(SEQ, "ch"),
        check_vma=False,
    )
```

```python
import functools

import jax
import jax.numpy as jnp
from jax import lax
from jax.experimental import pallas as pl
from jax.experimental.pallas import tpu as pltpu
from jax.sharding import Mesh, PartitionSpec as P

SEGS = 8
HALO = 16
LANES = 128
HISTORY = 8
WIDTH = 256
SEQ = ("z", "y", "x")
RING = 4
PARTS = 2
F32 = jnp.float32
BF16 = jnp.bfloat16
MIB = 1024 * 1024


def spread(row):
    return jnp.broadcast_to(row, (SEGS, row.shape[-1]))


def filtered_step(taps, now, one, two):
    return taps[0] * now + taps[1] * one + taps[2] * two


def tree_sum(parts):
    parts = list(parts)
    while len(parts) > 1:
        parts = [a + b for a, b in zip(parts[::2], parts[1::2])]
    return parts[0]


def stage_kernel(
    where_ref,
    own_ref,
    other_ref,
    w_ref,
    filt_ref,
    rates_ref,
    lhs_out,
    w_out,
    filt_out,
    rates_out,
    into_out,
    total_out,
    sems,
):
    rows, half = own_ref.shape
    core = lax.rem(where_ref[0], 2)
    mine = pl.multiple_of(core * half, half)
    theirs = pl.multiple_of((1 - core) * half, half)
    pairs = [
        (rates_ref, rates_out),
        (own_ref, lhs_out.at[:, pl.ds(mine, half)]),
        (other_ref, lhs_out.at[:, pl.ds(theirs, half)]),
        (filt_ref, filt_out),
        (w_ref.at[pl.ds(1, w_out.shape[0])], w_out),
    ]
    copies = [pltpu.make_async_copy(src, dst, sems.at[i]) for i, (src, dst) in enumerate(pairs)]
    for copy in copies:
        copy.start()
    copies[0].wait()
    rates = rates_out[...]
    rest, span, after = where_ref[0] // 2, rows, 0

    def decay(tokens):
        return jnp.exp(-rates * jnp.asarray(tokens, F32))

    for level in range(len(SEQ)):
        here = lax.rem(rest, RING)
        rest = rest // RING
        total_out[RING * level] = decay(span * (RING - 1 - here))
        for k in range(1, RING):
            inside = (k <= here).astype(F32)
            into_out[(RING - 1) * level + k - 1] = inside * decay(span * (k - 1) + after)
            place = lax.rem(here - k + RING, RING)
            total_out[RING * level + k] = decay(span * (RING - 1 - place))
        after = after + span * here
        span = span * RING
    for copy in copies[1:]:
        copy.wait()


def stage_call(where, own, other, weight, filt, rates):
    rows, half = own.shape
    vmem = pl.BlockSpec(memory_space=pltpu.VMEM)
    anywhere = pl.BlockSpec(memory_space=pl.ANY)
    inputs = [pltpu.with_memory_space_constraint(x, pltpu.HBM) for x in (own, weight, filt, rates)]
    return pl.pallas_call(
        stage_kernel,
        in_specs=[pl.BlockSpec(memory_space=pltpu.SMEM)] + [anywhere] * 5,
        out_specs=[vmem] * 6,
        out_shape=[
            pltpu.VMEM((rows, 2 * half), BF16),
            pltpu.VMEM((weight.shape[0] - 1, *weight.shape[1:]), BF16),
            pltpu.VMEM(filt.shape, F32),
            pltpu.VMEM(rates.shape, F32),
            pltpu.VMEM((len(SEQ) * (RING - 1), *rates.shape), F32),
            pltpu.VMEM((len(SEQ) * RING, *rates.shape), F32),
        ],
        scratch_shapes=[pltpu.SemaphoreType.DMA((5,))],
        compiler_params=pltpu.CompilerParams(vmem_limit_bytes=4 * MIB),
        name="stage",
    )(where, inputs[0], other, *inputs[1:])


def hold_segments(held, part, first, per):
    steps = held.shape[1] // SEGS - HISTORY
    pitch = steps + HISTORY
    for l in range(WIDTH // LANES):
        lanes = slice(l * LANES, (l + 1) * LANES)
        for g in range(first, first + per):
            row = (g - first) * steps + (0 if first else HALO)
            held[l, g * pitch + HISTORY : (g + 1) * pitch] = part[row : row + steps, lanes]
            if g == 0:
                held[l, :HISTORY] = part[row - HISTORY : row, lanes]
            if g + 1 < SEGS:
                held[l, (g + 1) * pitch : (g + 1) * pitch + HISTORY] = part[
                    row + steps - HISTORY : row + steps, lanes
                ]


def join_halo(where_ref, halo_ref, own_ref, other_ref):
    half = own_ref.shape[1]
    core = lax.rem(where_ref[0], 2)
    halo_ref[:, pl.ds(pl.multiple_of(core * half, half), half)] = own_ref[...]
    halo_ref[:, pl.ds(pl.multiple_of((1 - core) * half, half), half)] = other_ref[...]


def segment_rows(lhs_ref, halo_ref, first, per):
    steps = lhs_ref.shape[0] // SEGS
    rows = lhs_ref[first * steps : (first + per) * steps]
    return rows if first else jnp.concatenate([halo_ref[...], rows], axis=0)


def front_kernel(
    where_ref,
    lhs_ref,
    halo_own_ref,
    halo_other_ref,
    w_ref,
    wq_ref,
    filt_ref,
    rates_ref,
    source_ref,
    ends_ref,
    total_ref,
    staged_ref,
    halo_ref,
    proj_a,
    proj_b,
    sem,
):
    rows = lhs_ref.shape[0]
    steps = rows // SEGS
    pitch = steps + HISTORY
    modes = rates_ref.shape[0]
    streams = w_ref.shape[0]
    tiles = w_ref.shape[2] // WIDTH
    per = SEGS // 2
    proj = (proj_a, proj_b)

    stage = pltpu.make_async_copy(wq_ref.at[0], staged_ref, sem)
    stage.start()
    join_halo(where_ref, halo_ref, halo_own_ref, halo_other_ref)

    def projection(tile):
        held = proj[tile % 2]

        def piece(j, first):
            part = jnp.dot(
                segment_rows(lhs_ref, halo_ref, first, per),
                w_ref[j, :, tile * WIDTH : (tile + 1) * WIDTH],
                preferred_element_type=F32,
            )
            hold_segments(held.at[j], part, first, per)

        return [
            lambda j=j, first=first: piece(j, first)
            for j in range(streams)
            for first in range(0, SEGS, per)
        ]

    def recurrence(tile, size=4):
        held = proj[tile % 2]
        pieces = []
        for l in range(WIDTH // LANES):
            lanes = slice(tile * WIDTH + l * LANES, tile * WIDTH + (l + 1) * LANES)
            kept = {}

            def at(j, t, l=l):
                return held[j, l, pl.ds(HISTORY + t, SEGS, stride=pitch), :]

            def begin(kept=kept, lanes=lanes, at=at):
                kept["taps"] = [
                    [spread(filt_ref[a, j + 1 : j + 2, lanes]) for a in range(3)]
                    for j in range(streams)
                ]
                kept["decay"] = [spread(jnp.exp(-rates_ref[n : n + 1, lanes])) for n in range(modes)]
                kept["one"] = [at(j, -1) for j in range(streams)]
                kept["two"] = [at(j, -2) for j in range(streams)]
                kept["state"] = [jnp.zeros((SEGS, LANES), F32)] * modes

            def advance(t0, kept=kept, lanes=lanes, at=at):
                for t in range(t0, t0 + size):
                    now = [at(j, t) for j in range(streams)]
                    k, v = [
                        filtered_step(*terms)
                        for terms in zip(kept["taps"], now, kept["one"], kept["two"])
                    ]
                    kept["one"], kept["two"] = now, kept["one"]
                    source = k * v
                    kept["state"] = [d * s + source for d, s in zip(kept["decay"], kept["state"])]
                    source_ref[t * SEGS : (t + 1) * SEGS, lanes] = source

            def finish(kept=kept, lanes=lanes):
                seg = lax.broadcasted_iota(jnp.int32, (SEGS, LANES), 0)
                later = (SEGS - 1 - seg).astype(F32) * float(steps)
                for n, state in enumerate(kept["state"]):
                    ends_ref[n * SEGS : (n + 1) * SEGS, lanes] = state
                    weight = jnp.exp(-spread(rates_ref[n : n + 1, lanes]) * later)
                    total_ref[n : n + 1, lanes] = jnp.sum(state * weight, axis=0, keepdims=True)

            pieces += [begin]
            pieces += [lambda t0=t0, advance=advance: advance(t0) for t0 in range(0, steps, size)]
            pieces += [finish]
        return pieces

    for work in projection(0):
        work()
    for tile in range(tiles):
        slow = projection(tile + 1) if tile + 1 < tiles else [lambda: None]
        fast = recurrence(tile)
        done = 0
        for i, work in enumerate(slow):
            work()
            upto = (i + 1) * len(fast) // len(slow)
            for step in fast[done:upto]:
                step()
            done = upto
    stage.wait()


def front_call(where, lhs, halo_own, halo_other, staged, weight, filt, rates):
    rows, full = lhs.shape
    streams, _, channels = staged.shape
    modes = rates.shape[0]
    vmem = pl.BlockSpec(memory_space=pltpu.VMEM)
    held = pltpu.VMEM((streams, WIDTH // LANES, rows + SEGS * HISTORY, LANES), F32)
    return pl.pallas_call(
        front_kernel,
        in_specs=[pl.BlockSpec(memory_space=pltpu.SMEM)]
        + [vmem] * 4
        + [pl.BlockSpec(memory_space=pl.ANY)]
        + [vmem] * 2,
        out_specs=[vmem] * 4,
        out_shape=[
            pltpu.VMEM((rows, channels), F32),
            pltpu.VMEM((modes * SEGS, channels), F32),
            pltpu.VMEM((modes, channels), F32),
            pltpu.VMEM((full, channels), BF16),
        ],
        scratch_shapes=[pltpu.VMEM((HALO, full), BF16), held, held, pltpu.SemaphoreType.DMA],
        compiler_params=pltpu.CompilerParams(vmem_limit_bytes=10 * MIB),
        name="front",
    )(
        where,
        lhs,
        halo_own,
        halo_other,
        staged,
        pltpu.with_memory_space_constraint(weight, pltpu.HBM),
        filt,
        rates,
    )


def query_kernel(where_ref, lhs_ref, halo_own_ref, halo_other_ref, w_ref, filt_ref, query_ref, halo_ref, held):
    steps = lhs_ref.shape[0] // SEGS
    pitch = steps + HISTORY
    per = SEGS // 2
    join_halo(where_ref, halo_ref, halo_own_ref, halo_other_ref)
    for tile in range(w_ref.shape[1] // WIDTH):
        for first in range(0, SEGS, per):
            part = jnp.dot(
                segment_rows(lhs_ref, halo_ref, first, per),
                w_ref[:, tile * WIDTH : (tile + 1) * WIDTH],
                preferred_element_type=F32,
            )
            hold_segments(held.at[tile], part, first, per)
        for l in range(WIDTH // LANES):
            lanes = slice(tile * WIDTH + l * LANES, tile * WIDTH + (l + 1) * LANES)
            taps = [spread(filt_ref[a, 0:1, lanes]) for a in range(3)]

            def at(t, tile=tile, l=l):
                return held[tile, l, pl.ds(HISTORY + t, SEGS, stride=pitch), :]

            one, two = at(-1), at(-2)
            for t in range(steps):
                now = at(t)
                query_ref[t * SEGS : (t + 1) * SEGS, lanes] = filtered_step(taps, now, one, two)
                one, two = now, one


def query_call(where, lhs, halo_own, halo_other, weight, filt):
    rows, full = lhs.shape
    channels = weight.shape[1]
    vmem = pl.BlockSpec(memory_space=pltpu.VMEM)
    args = [
        pltpu.with_memory_space_constraint(x, pltpu.VMEM)
        for x in (lhs, halo_own, halo_other, weight, filt)
    ]
    return pl.pallas_call(
        query_kernel,
        in_specs=[pl.BlockSpec(memory_space=pltpu.SMEM)] + [vmem] * 5,
        out_specs=vmem,
        out_shape=pltpu.VMEM((rows, channels), F32),
        scratch_shapes=[
            pltpu.VMEM((HALO, full), BF16),
            pltpu.VMEM((channels // WIDTH, WIDTH // LANES, rows + SEGS * HISTORY, LANES), F32),
        ],
        compiler_params=pltpu.CompilerParams(vmem_limit_bytes=6 * MIB),
        cost_estimate=pl.CostEstimate(
            flops=2 * (rows + HALO) * full * channels, transcendentals=0, bytes_accessed=0
        ),
        name="query",
    )(where, *args)


def local_kernel(first, source_ref, ends_ref, rates_ref, gain_ref, local_ref, base_ref, factor_ref):
    rows, channels = local_ref.shape
    steps = rows // SEGS
    modes = rates_ref.shape[0]
    seg = lax.broadcasted_iota(jnp.int32, (SEGS, LANES), 0)
    for i in range(channels // LANES):
        lanes = slice(first + i * LANES, first + (i + 1) * LANES)
        here = slice(i * LANES, (i + 1) * LANES)
        rates = [spread(rates_ref[n : n + 1, lanes]) for n in range(modes)]
        gains = [spread(gain_ref[n : n + 1, lanes]) for n in range(modes)]
        for n in range(modes):
            mode = slice(n * SEGS, (n + 1) * SEGS)
            state = jnp.where(seg >= 1, pltpu.roll(ends_ref[mode, lanes], 1, 0), 0.0)
            for hop in (1, 2, 4):
                earlier = pltpu.roll(state, hop, 0) * jnp.exp(-rates[n] * float(steps * hop))
                state = state + jnp.where(seg >= hop, earlier, 0.0)
            base_ref[mode, here] = gains[n] * state
            factor_ref[mode, here] = gains[n] * jnp.exp(-rates[n] * (seg * steps).astype(F32))
        decays = [jnp.exp(-rate) for rate in rates]
        states = [jnp.zeros((SEGS, LANES), F32)] * modes
        for t in range(steps):
            row = slice(t * SEGS, (t + 1) * SEGS)
            source = source_ref[row, lanes]
            states = [d * s + source for d, s in zip(decays, states)]
            local_ref[row, here] = tree_sum([g * s for g, s in zip(gains, states)])


def local_call(source, ends, rates, gain, part):
    rows, channels = source.shape
    wide = channels // PARTS
    vmem = pl.BlockSpec(memory_space=pltpu.VMEM)
    args = [pltpu.with_memory_space_constraint(x, pltpu.VMEM) for x in (source, ends, rates, gain)]
    return pl.pallas_call(
        functools.partial(local_kernel, part * wide),
        in_specs=[vmem] * 4,
        out_specs=[vmem] * 3,
        out_shape=[
            pltpu.VMEM((rows, wide), F32),
            pltpu.VMEM((ends.shape[0], wide), F32),
            pltpu.VMEM((ends.shape[0], wide), F32),
        ],
        compiler_params=pltpu.CompilerParams(vmem_limit_bytes=4 * MIB),
        cost_estimate=pl.CostEstimate(
            flops=4 * rates.shape[0] * rows * wide, transcendentals=0, bytes_accessed=0
        ),
        name="local",
    )(*args)


def hidden_kernel(into_ref, query_ref, rates_ref, *refs):
    hidden_ref = refs[-1]
    rows, channels = query_ref.shape
    modes = rates_ref.shape[0]
    wide = channels // PARTS
    for i in range(channels // LANES):
        lanes = slice(i * LANES, (i + 1) * LANES)
        part = i * LANES // wide
        local_ref, base_ref, factor_ref = refs[3 * part : 3 * part + 3]
        here = slice(lanes.start - part * wide, lanes.stop - part * wide)
        decays, leads = [], []
        for n in range(modes):
            mode = slice(n * SEGS, (n + 1) * SEGS)
            decays.append(spread(jnp.exp(-rates_ref[n : n + 1, lanes])))
            incoming = spread(into_ref[n : n + 1, lanes])
            leads.append(base_ref[mode, here] + factor_ref[mode, here] * incoming)
        for t in range(0, rows, 2 * SEGS):
            halves = []
            for row in (slice(t, t + SEGS), slice(t + SEGS, t + 2 * SEGS)):
                leads = [d * s for d, s in zip(decays, leads)]
                halves.append(query_ref[row, lanes] * (local_ref[row, here] + tree_sum(leads)))
            hidden_ref[t : t + 2 * SEGS, lanes] = jnp.concatenate(halves, axis=0).astype(BF16)


def hidden_call(into, query, rates, parts):
    vmem = pl.BlockSpec(memory_space=pltpu.VMEM)
    args = [
        pltpu.with_memory_space_constraint(x, pltpu.VMEM)
        for x in (into, query, rates, *(ref for part in parts for ref in part))
    ]
    return pl.pallas_call(
        hidden_kernel,
        in_specs=[vmem] * len(args),
        out_specs=vmem,
        out_shape=pltpu.VMEM(query.shape, BF16),
        compiler_params=pltpu.CompilerParams(vmem_limit_bytes=4 * MIB),
        name="hidden",
    )(*args)


def product_kernel(where_ref, hidden_ref, w_ref, w_other_ref, part_ref, staged_ref, mine_ref, sems):
    columns = part_ref.shape[1]
    lanes = pl.ds(pl.multiple_of(lax.rem(where_ref[0], 2) * columns, columns), columns)
    mine = pltpu.make_async_copy(w_ref.at[:, lanes], mine_ref, sems.at[0])
    theirs = pltpu.make_async_copy(w_other_ref.at[:, lanes], staged_ref, sems.at[1])
    mine.start()
    theirs.start()
    mine.wait()
    part_ref[...] = jnp.dot(hidden_ref[...], mine_ref[...], preferred_element_type=F32)
    theirs.wait()


def product_call(where, hidden, weight, weight_other):
    rows, channels = hidden.shape
    columns = weight.shape[1] // 2
    vmem = pl.BlockSpec(memory_space=pltpu.VMEM)
    anywhere = pl.BlockSpec(memory_space=pl.ANY)
    return pl.pallas_call(
        product_kernel,
        in_specs=[pl.BlockSpec(memory_space=pltpu.SMEM), vmem, anywhere, anywhere],
        out_specs=[vmem] * 2,
        out_shape=[pltpu.VMEM((rows, columns), F32), pltpu.VMEM((channels, columns), BF16)],
        scratch_shapes=[pltpu.VMEM((channels, columns), BF16), pltpu.SemaphoreType.DMA((2,))],
        compiler_params=pltpu.CompilerParams(vmem_limit_bytes=8 * MIB),
        name="product",
    )(where, hidden, weight, weight_other)


def output_kernel(part_ref, other_ref, w_ref, out_ref, acc_ref, rows_ref, sems):
    rows, columns = part_ref.shape
    steps = rows // SEGS
    copies = []
    for tile in range(columns // WIDTH):
        lanes = slice(tile * WIDTH, (tile + 1) * WIDTH)
        part = part_ref[:, lanes] + jnp.dot(
            other_ref[...], w_ref[:, lanes], preferred_element_type=F32
        )
        for l in range(WIDTH // LANES):
            acc_ref[tile, l] = part[:, l * LANES : (l + 1) * LANES]
            for j in range(SEGS):
                rows_ref[
                    j * steps : (j + 1) * steps,
                    tile * WIDTH + l * LANES : tile * WIDTH + (l + 1) * LANES,
                ] = acc_ref[tile, l, pl.ds(j, steps, stride=SEGS), :]
        copies.append(pltpu.make_async_copy(rows_ref.at[:, lanes], out_ref.at[:, lanes], sems.at[tile]))
        copies[-1].start()
    for copy in copies:
        copy.wait()


def output_call(part, other, weight):
    rows, columns = part.shape
    vmem = pl.BlockSpec(memory_space=pltpu.VMEM)
    args = [pltpu.with_memory_space_constraint(x, pltpu.VMEM) for x in (part, other, weight)]
    return pl.pallas_call(
        output_kernel,
        in_specs=[vmem] * 3,
        out_specs=pl.BlockSpec(memory_space=pl.ANY),
        out_shape=jax.ShapeDtypeStruct((rows, columns), F32),
        scratch_shapes=[
            pltpu.VMEM((columns // WIDTH, WIDTH // LANES, rows, LANES), F32),
            pltpu.VMEM((rows, columns), F32),
            pltpu.SemaphoreType.DMA((columns // WIDTH,)),
        ],
        compiler_params=pltpu.CompilerParams(vmem_limit_bytes=8 * MIB),
        name="output",
    )(*args)


def swapped(x):
    return lax.ppermute(x, "ch", [(0, 1), (1, 0)])


def from_before(x):
    count = RING**3
    return lax.ppermute(x, SEQ, [(i, i + 1) for i in range(count - 1)])


def round_the_ring(state, axis):
    sent = state.astype(BF16)
    return [
        lax.ppermute(sent, axis, [(i, (i + k) % RING) for i in range(RING)])
        for k in range(1, RING)
    ]


def on_device(tokens, in_weight, short_filter, residues, rates, out_weight):
    rows = tokens.shape[0]
    where = lax.axis_index((*SEQ, "ch")).astype(jnp.int32).reshape(1)
    weight = in_weight.transpose(1, 0, 2)
    rates = rates.T
    gain = residues.T * jnp.sqrt(1.0 - jnp.exp(-2.0 * rates))

    halo_own = from_before(tokens[rows - HALO :])
    lhs, staged, filt, rates, into_weights, total_weights = stage_call(
        where, tokens, swapped(tokens), weight, short_filter, rates
    )
    halo_own, lhs, out_weight = lax.optimization_barrier((halo_own, lhs, out_weight))
    halo_other = swapped(halo_own)
    lhs, halo_other, out_weight = lax.optimization_barrier((lhs, halo_other, out_weight))
    out_weight_other = swapped(out_weight)
    source, ends, total, query_weight = front_call(
        where, lhs, halo_own, halo_other, staged, weight, filt, rates
    )
    beside = [
        query_call(where, lhs, halo_own, halo_other, query_weight, filt),
        *[local_call(source, ends, rates, gain, part) for part in range(PARTS)],
    ]

    into = 0.0
    for level, axis in enumerate(reversed(SEQ)):
        arrived = round_the_ring(total, axis)
        beside[level], *arrived = lax.optimization_barrier((beside[level], *arrived))
        total = total_weights[RING * level] * total
        for k, part in enumerate(arrived):
            part = part.astype(F32)
            into = into + into_weights[(RING - 1) * level + k] * part
            total = total + total_weights[RING * level + k + 1] * part

    hidden = hidden_call(into, beside[0], rates, beside[1:])
    part, partner_weight = product_call(where, hidden, out_weight, out_weight_other)
    return output_call(part, swapped(hidden), partner_weight)


def solution(mesh):
    cube = Mesh(mesh.devices.reshape(RING, RING, RING, 2), (*SEQ, "ch"))
    return jax.shard_map(
        on_device,
        mesh=cube,
        in_specs=(
            P(SEQ, "ch"),
            P(None, None, "ch"),
            P(None, None, "ch"),
            P("ch", None),
            P("ch", None),
            P("ch", None),
        ),
        out_specs=P(SEQ, "ch"),
        check_vma=False,
    )
```

```python
import functools

import jax
import jax.numpy as jnp
from jax import lax
from jax.experimental import pallas as pl
from jax.experimental.pallas import tpu as pltpu
from jax.sharding import Mesh, PartitionSpec as P

SEGS = 8
HALO = 16
LANES = 128
HISTORY = 8
WIDTH = 256
SEQ = ("z", "y", "x")
RING = 4
PARTS = 2
F32 = jnp.float32
BF16 = jnp.bfloat16
MIB = 1024 * 1024


def spread(row):
    return jnp.broadcast_to(row, (SEGS, row.shape[-1]))


def filtered_step(taps, now, one, two):
    return taps[0] * now + taps[1] * one + taps[2] * two


def tree_sum(parts):
    parts = list(parts)
    while len(parts) > 1:
        parts = [a + b for a, b in zip(parts[::2], parts[1::2])]
    return parts[0]


def stage_kernel(
    where_ref,
    own_ref,
    other_ref,
    w_ref,
    filt_ref,
    rates_ref,
    lhs_out,
    w_out,
    filt_out,
    rates_out,
    into_out,
    total_out,
    sems,
):
    rows, half = own_ref.shape
    core = lax.rem(where_ref[0], 2)
    mine = pl.multiple_of(core * half, half)
    theirs = pl.multiple_of((1 - core) * half, half)
    pairs = [
        (rates_ref, rates_out),
        (own_ref, lhs_out.at[:, pl.ds(mine, half)]),
        (other_ref, lhs_out.at[:, pl.ds(theirs, half)]),
        (filt_ref, filt_out),
        (w_ref.at[pl.ds(1, w_out.shape[0])], w_out),
    ]
    copies = [pltpu.make_async_copy(src, dst, sems.at[i]) for i, (src, dst) in enumerate(pairs)]
    for copy in copies:
        copy.start()
    copies[0].wait()
    rates = rates_out[...]
    rest, span, after = where_ref[0] // 2, rows, 0

    def decay(tokens):
        return jnp.exp(-rates * jnp.asarray(tokens, F32))

    for level in range(len(SEQ)):
        here = lax.rem(rest, RING)
        rest = rest // RING
        total_out[RING * level] = decay(span * (RING - 1 - here))
        for k in range(1, RING):
            inside = (k <= here).astype(F32)
            into_out[(RING - 1) * level + k - 1] = inside * decay(span * (k - 1) + after)
            place = lax.rem(here - k + RING, RING)
            total_out[RING * level + k] = decay(span * (RING - 1 - place))
        after = after + span * here
        span = span * RING
    for copy in copies[1:]:
        copy.wait()


def stage_call(where, own, other, weight, filt, rates):
    rows, half = own.shape
    vmem = pl.BlockSpec(memory_space=pltpu.VMEM)
    anywhere = pl.BlockSpec(memory_space=pl.ANY)
    inputs = [pltpu.with_memory_space_constraint(x, pltpu.HBM) for x in (own, weight, filt, rates)]
    return pl.pallas_call(
        stage_kernel,
        in_specs=[pl.BlockSpec(memory_space=pltpu.SMEM)] + [anywhere] * 5,
        out_specs=[vmem] * 6,
        out_shape=[
            pltpu.VMEM((rows, 2 * half), BF16),
            pltpu.VMEM((weight.shape[0] - 1, *weight.shape[1:]), BF16),
            pltpu.VMEM(filt.shape, F32),
            pltpu.VMEM(rates.shape, F32),
            pltpu.VMEM((len(SEQ) * (RING - 1), *rates.shape), F32),
            pltpu.VMEM((len(SEQ) * RING, *rates.shape), F32),
        ],
        scratch_shapes=[pltpu.SemaphoreType.DMA((5,))],
        compiler_params=pltpu.CompilerParams(vmem_limit_bytes=4 * MIB),
        name="stage",
    )(where, inputs[0], other, *inputs[1:])


def hold_segments(held, part, first, per):
    steps = held.shape[1] // SEGS - HISTORY
    pitch = steps + HISTORY
    for l in range(WIDTH // LANES):
        lanes = slice(l * LANES, (l + 1) * LANES)
        for g in range(first, first + per):
            row = (g - first) * steps + (0 if first else HALO)
            held[l, g * pitch + HISTORY : (g + 1) * pitch] = part[row : row + steps, lanes]
            if g == 0:
                held[l, :HISTORY] = part[row - HISTORY : row, lanes]
            if g + 1 < SEGS:
                held[l, (g + 1) * pitch : (g + 1) * pitch + HISTORY] = part[
                    row + steps - HISTORY : row + steps, lanes
                ]


def join_halo(where_ref, halo_ref, own_ref, other_ref):
    half = own_ref.shape[1]
    core = lax.rem(where_ref[0], 2)
    halo_ref[:, pl.ds(pl.multiple_of(core * half, half), half)] = own_ref[...]
    halo_ref[:, pl.ds(pl.multiple_of((1 - core) * half, half), half)] = other_ref[...]


def segment_rows(lhs_ref, halo_ref, first, per):
    steps = lhs_ref.shape[0] // SEGS
    rows = lhs_ref[first * steps : (first + per) * steps]
    return rows if first else jnp.concatenate([halo_ref[...], rows], axis=0)


def front_kernel(
    where_ref,
    lhs_ref,
    halo_own_ref,
    halo_other_ref,
    w_ref,
    wq_ref,
    wout_ref,
    filt_ref,
    rates_ref,
    source_ref,
    ends_ref,
    total_ref,
    staged_ref,
    mine_ref,
    theirs_ref,
    halo_ref,
    proj_a,
    proj_b,
    sems,
):
    rows = lhs_ref.shape[0]
    steps = rows // SEGS
    pitch = steps + HISTORY
    modes = rates_ref.shape[0]
    streams = w_ref.shape[0]
    tiles = w_ref.shape[2] // WIDTH
    per = SEGS // 2
    proj = (proj_a, proj_b)

    columns = mine_ref.shape[1]
    core = lax.rem(where_ref[0], 2)
    mine = pl.ds(pl.multiple_of(core * columns, columns), columns)
    theirs = pl.ds(pl.multiple_of((1 - core) * columns, columns), columns)
    stages = [
        pltpu.make_async_copy(src, dst, sems.at[i])
        for i, (src, dst) in enumerate(
            (
                (wq_ref.at[0], staged_ref),
                (wout_ref.at[:, theirs], theirs_ref),
                (wout_ref.at[:, mine], mine_ref),
            )
        )
    ]
    for stage in stages:
        stage.start()
    join_halo(where_ref, halo_ref, halo_own_ref, halo_other_ref)

    def projection(tile):
        held = proj[tile % 2]

        def piece(j, first):
            part = jnp.dot(
                segment_rows(lhs_ref, halo_ref, first, per),
                w_ref[j, :, tile * WIDTH : (tile + 1) * WIDTH],
                preferred_element_type=F32,
            )
            hold_segments(held.at[j], part, first, per)

        return [
            lambda j=j, first=first: piece(j, first)
            for j in range(streams)
            for first in range(0, SEGS, per)
        ]

    def recurrence(tile, size=4):
        held = proj[tile % 2]
        pieces = []
        for l in range(WIDTH // LANES):
            lanes = slice(tile * WIDTH + l * LANES, tile * WIDTH + (l + 1) * LANES)
            kept = {}

            def at(j, t, l=l):
                return held[j, l, pl.ds(HISTORY + t, SEGS, stride=pitch), :]

            def begin(kept=kept, lanes=lanes, at=at):
                kept["taps"] = [
                    [spread(filt_ref[a, j + 1 : j + 2, lanes]) for a in range(3)]
                    for j in range(streams)
                ]
                kept["decay"] = [spread(jnp.exp(-rates_ref[n : n + 1, lanes])) for n in range(modes)]
                kept["one"] = [at(j, -1) for j in range(streams)]
                kept["two"] = [at(j, -2) for j in range(streams)]
                kept["state"] = [jnp.zeros((SEGS, LANES), F32)] * modes

            def advance(t0, kept=kept, lanes=lanes, at=at):
                for t in range(t0, t0 + size):
                    now = [at(j, t) for j in range(streams)]
                    k, v = [
                        filtered_step(*terms)
                        for terms in zip(kept["taps"], now, kept["one"], kept["two"])
                    ]
                    kept["one"], kept["two"] = now, kept["one"]
                    source = k * v
                    kept["state"] = [d * s + source for d, s in zip(kept["decay"], kept["state"])]
                    source_ref[t * SEGS : (t + 1) * SEGS, lanes] = source

            def finish(kept=kept, lanes=lanes):
                seg = lax.broadcasted_iota(jnp.int32, (SEGS, LANES), 0)
                later = (SEGS - 1 - seg).astype(F32) * float(steps)
                for n, state in enumerate(kept["state"]):
                    ends_ref[n * SEGS : (n + 1) * SEGS, lanes] = state
                    weight = jnp.exp(-spread(rates_ref[n : n + 1, lanes]) * later)
                    total_ref[n : n + 1, lanes] = jnp.sum(state * weight, axis=0, keepdims=True)

            pieces += [begin]
            pieces += [lambda t0=t0, advance=advance: advance(t0) for t0 in range(0, steps, size)]
            pieces += [finish]
        return pieces

    for work in projection(0):
        work()
    for tile in range(tiles):
        slow = projection(tile + 1) if tile + 1 < tiles else [lambda: None]
        fast = recurrence(tile)
        done = 0
        for i, work in enumerate(slow):
            work()
            upto = (i + 1) * len(fast) // len(slow)
            for step in fast[done:upto]:
                step()
            done = upto
    for stage in stages:
        stage.wait()


def front_call(where, lhs, halo_own, halo_other, staged, weight, out_weight, filt, rates):
    rows, full = lhs.shape
    streams, _, channels = staged.shape
    modes = rates.shape[0]
    vmem = pl.BlockSpec(memory_space=pltpu.VMEM)
    held = pltpu.VMEM((streams, WIDTH // LANES, rows + SEGS * HISTORY, LANES), F32)
    return pl.pallas_call(
        front_kernel,
        in_specs=[pl.BlockSpec(memory_space=pltpu.SMEM)]
        + [vmem] * 4
        + [pl.BlockSpec(memory_space=pl.ANY)] * 2
        + [vmem] * 2,
        out_specs=[vmem] * 6,
        out_shape=[
            pltpu.VMEM((rows, channels), F32),
            pltpu.VMEM((modes * SEGS, channels), F32),
            pltpu.VMEM((modes, channels), F32),
            pltpu.VMEM((full, channels), BF16),
            pltpu.VMEM((channels, out_weight.shape[1] // 2), BF16),
            pltpu.VMEM((channels, out_weight.shape[1] // 2), BF16),
        ],
        scratch_shapes=[pltpu.VMEM((HALO, full), BF16), held, held, pltpu.SemaphoreType.DMA((3,))],
        compiler_params=pltpu.CompilerParams(vmem_limit_bytes=10 * MIB),
        name="front",
    )(
        where,
        lhs,
        halo_own,
        halo_other,
        staged,
        pltpu.with_memory_space_constraint(weight, pltpu.HBM),
        pltpu.with_memory_space_constraint(out_weight, pltpu.HBM),
        filt,
        rates,
    )


def query_kernel(where_ref, lhs_ref, halo_own_ref, halo_other_ref, w_ref, filt_ref, query_ref, halo_ref, held):
    steps = lhs_ref.shape[0] // SEGS
    pitch = steps + HISTORY
    per = SEGS // 2
    join_halo(where_ref, halo_ref, halo_own_ref, halo_other_ref)
    for tile in range(w_ref.shape[1] // WIDTH):
        for first in range(0, SEGS, per):
            part = jnp.dot(
                segment_rows(lhs_ref, halo_ref, first, per),
                w_ref[:, tile * WIDTH : (tile + 1) * WIDTH],
                preferred_element_type=F32,
            )
            hold_segments(held.at[tile], part, first, per)
        for l in range(WIDTH // LANES):
            lanes = slice(tile * WIDTH + l * LANES, tile * WIDTH + (l + 1) * LANES)
            taps = [spread(filt_ref[a, 0:1, lanes]) for a in range(3)]

            def at(t, tile=tile, l=l):
                return held[tile, l, pl.ds(HISTORY + t, SEGS, stride=pitch), :]

            one, two = at(-1), at(-2)
            for t in range(steps):
                now = at(t)
                query_ref[t * SEGS : (t + 1) * SEGS, lanes] = filtered_step(taps, now, one, two)
                one, two = now, one


def query_call(where, lhs, halo_own, halo_other, weight, filt):
    rows, full = lhs.shape
    channels = weight.shape[1]
    vmem = pl.BlockSpec(memory_space=pltpu.VMEM)
    args = [
        pltpu.with_memory_space_constraint(x, pltpu.VMEM)
        for x in (lhs, halo_own, halo_other, weight, filt)
    ]
    return pl.pallas_call(
        query_kernel,
        in_specs=[pl.BlockSpec(memory_space=pltpu.SMEM)] + [vmem] * 5,
        out_specs=vmem,
        out_shape=pltpu.VMEM((rows, channels), F32),
        scratch_shapes=[
            pltpu.VMEM((HALO, full), BF16),
            pltpu.VMEM((channels // WIDTH, WIDTH // LANES, rows + SEGS * HISTORY, LANES), F32),
        ],
        compiler_params=pltpu.CompilerParams(vmem_limit_bytes=6 * MIB),
        cost_estimate=pl.CostEstimate(
            flops=2 * (rows + HALO) * full * channels, transcendentals=0, bytes_accessed=0
        ),
        name="query",
    )(where, *args)


def local_kernel(first, source_ref, ends_ref, rates_ref, gain_ref, local_ref, base_ref, factor_ref):
    rows, channels = local_ref.shape
    steps = rows // SEGS
    modes = rates_ref.shape[0]
    seg = lax.broadcasted_iota(jnp.int32, (SEGS, LANES), 0)
    for i in range(channels // LANES):
        lanes = slice(first + i * LANES, first + (i + 1) * LANES)
        here = slice(i * LANES, (i + 1) * LANES)
        rates = [spread(rates_ref[n : n + 1, lanes]) for n in range(modes)]
        gains = [spread(gain_ref[n : n + 1, lanes]) for n in range(modes)]
        for n in range(modes):
            mode = slice(n * SEGS, (n + 1) * SEGS)
            state = jnp.where(seg >= 1, pltpu.roll(ends_ref[mode, lanes], 1, 0), 0.0)
            for hop in (1, 2, 4):
                earlier = pltpu.roll(state, hop, 0) * jnp.exp(-rates[n] * float(steps * hop))
                state = state + jnp.where(seg >= hop, earlier, 0.0)
            base_ref[mode, here] = gains[n] * state
            factor_ref[mode, here] = gains[n] * jnp.exp(-rates[n] * (seg * steps).astype(F32))
        decays = [jnp.exp(-rate) for rate in rates]
        states = [jnp.zeros((SEGS, LANES), F32)] * modes
        for t in range(steps):
            row = slice(t * SEGS, (t + 1) * SEGS)
            source = source_ref[row, lanes]
            states = [d * s + source for d, s in zip(decays, states)]
            local_ref[row, here] = tree_sum([g * s for g, s in zip(gains, states)])


def local_call(source, ends, rates, gain, part):
    rows, channels = source.shape
    wide = channels // PARTS
    vmem = pl.BlockSpec(memory_space=pltpu.VMEM)
    args = [pltpu.with_memory_space_constraint(x, pltpu.VMEM) for x in (source, ends, rates, gain)]
    return pl.pallas_call(
        functools.partial(local_kernel, part * wide),
        in_specs=[vmem] * 4,
        out_specs=[vmem] * 3,
        out_shape=[
            pltpu.VMEM((rows, wide), F32),
            pltpu.VMEM((ends.shape[0], wide), F32),
            pltpu.VMEM((ends.shape[0], wide), F32),
        ],
        compiler_params=pltpu.CompilerParams(vmem_limit_bytes=4 * MIB),
        cost_estimate=pl.CostEstimate(
            flops=4 * rates.shape[0] * rows * wide, transcendentals=0, bytes_accessed=0
        ),
        name="local",
    )(*args)


def hidden_kernel(into_ref, query_ref, rates_ref, *refs):
    hidden_ref = refs[-1]
    rows, channels = query_ref.shape
    modes = rates_ref.shape[0]
    wide = channels // PARTS
    for i in range(channels // LANES):
        lanes = slice(i * LANES, (i + 1) * LANES)
        part = i * LANES // wide
        local_ref, base_ref, factor_ref = refs[3 * part : 3 * part + 3]
        here = slice(lanes.start - part * wide, lanes.stop - part * wide)
        decays, leads = [], []
        for n in range(modes):
            mode = slice(n * SEGS, (n + 1) * SEGS)
            decays.append(spread(jnp.exp(-rates_ref[n : n + 1, lanes])))
            incoming = spread(into_ref[n : n + 1, lanes])
            leads.append(base_ref[mode, here] + factor_ref[mode, here] * incoming)
        for t in range(0, rows, 2 * SEGS):
            halves = []
            for row in (slice(t, t + SEGS), slice(t + SEGS, t + 2 * SEGS)):
                leads = [d * s for d, s in zip(decays, leads)]
                halves.append(query_ref[row, lanes] * (local_ref[row, here] + tree_sum(leads)))
            hidden_ref[t : t + 2 * SEGS, lanes] = jnp.concatenate(halves, axis=0).astype(BF16)


def hidden_call(into, query, rates, parts):
    vmem = pl.BlockSpec(memory_space=pltpu.VMEM)
    args = [
        pltpu.with_memory_space_constraint(x, pltpu.VMEM)
        for x in (into, query, rates, *(ref for part in parts for ref in part))
    ]
    return pl.pallas_call(
        hidden_kernel,
        in_specs=[vmem] * len(args),
        out_specs=vmem,
        out_shape=pltpu.VMEM(query.shape, BF16),
        compiler_params=pltpu.CompilerParams(vmem_limit_bytes=4 * MIB),
        name="hidden",
    )(*args)


def product_kernel(hidden_ref, w_ref, part_ref):
    for tile in range(part_ref.shape[1] // WIDTH):
        lanes = slice(tile * WIDTH, (tile + 1) * WIDTH)
        part_ref[:, lanes] = jnp.dot(
            hidden_ref[...], w_ref[:, lanes], preferred_element_type=F32
        )


def product_call(hidden, weight):
    vmem = pl.BlockSpec(memory_space=pltpu.VMEM)
    args = [pltpu.with_memory_space_constraint(x, pltpu.VMEM) for x in (hidden, weight)]
    return pl.pallas_call(
        product_kernel,
        in_specs=[vmem] * 2,
        out_specs=vmem,
        out_shape=pltpu.VMEM((hidden.shape[0], weight.shape[1]), F32),
        compiler_params=pltpu.CompilerParams(vmem_limit_bytes=4 * MIB),
        name="product",
    )(*args)


def output_kernel(part_ref, other_ref, w_ref, out_ref, acc_ref, rows_ref, sems):
    rows, columns = part_ref.shape
    steps = rows // SEGS
    copies = []
    for tile in range(columns // WIDTH):
        lanes = slice(tile * WIDTH, (tile + 1) * WIDTH)
        part = part_ref[:, lanes] + jnp.dot(
            other_ref[...], w_ref[:, lanes], preferred_element_type=F32
        )
        for l in range(WIDTH // LANES):
            acc_ref[tile, l] = part[:, l * LANES : (l + 1) * LANES]
            for j in range(SEGS):
                rows_ref[
                    j * steps : (j + 1) * steps,
                    tile * WIDTH + l * LANES : tile * WIDTH + (l + 1) * LANES,
                ] = acc_ref[tile, l, pl.ds(j, steps, stride=SEGS), :]
        copies.append(pltpu.make_async_copy(rows_ref.at[:, lanes], out_ref.at[:, lanes], sems.at[tile]))
        copies[-1].start()
    for copy in copies:
        copy.wait()


def output_call(part, other, weight):
    rows, columns = part.shape
    vmem = pl.BlockSpec(memory_space=pltpu.VMEM)
    args = [pltpu.with_memory_space_constraint(x, pltpu.VMEM) for x in (part, other, weight)]
    return pl.pallas_call(
        output_kernel,
        in_specs=[vmem] * 3,
        out_specs=pl.BlockSpec(memory_space=pl.ANY),
        out_shape=jax.ShapeDtypeStruct((rows, columns), F32),
        scratch_shapes=[
            pltpu.VMEM((columns // WIDTH, WIDTH // LANES, rows, LANES), F32),
            pltpu.VMEM((rows, columns), F32),
            pltpu.SemaphoreType.DMA((columns // WIDTH,)),
        ],
        compiler_params=pltpu.CompilerParams(vmem_limit_bytes=8 * MIB),
        name="output",
    )(*args)


def swapped(x):
    return lax.ppermute(x, "ch", [(0, 1), (1, 0)])


def from_before(x):
    count = RING**3
    return lax.ppermute(x, SEQ, [(i, i + 1) for i in range(count - 1)])


def round_the_ring(state, axis):
    sent = state.astype(BF16)
    return [
        lax.ppermute(sent, axis, [(i, (i + k) % RING) for i in range(RING)])
        for k in range(1, RING)
    ]


def on_device(tokens, in_weight, short_filter, residues, rates, out_weight):
    rows = tokens.shape[0]
    where = lax.axis_index((*SEQ, "ch")).astype(jnp.int32).reshape(1)
    weight = in_weight.transpose(1, 0, 2)
    rates = rates.T
    gain = residues.T * jnp.sqrt(1.0 - jnp.exp(-2.0 * rates))

    halo_own = from_before(tokens[rows - HALO :])
    lhs, staged, filt, rates, into_weights, total_weights = stage_call(
        where, tokens, swapped(tokens), weight, short_filter, rates
    )
    halo_own, lhs = lax.optimization_barrier((halo_own, lhs))
    halo_other = swapped(halo_own)
    source, ends, total, query_weight, mine, theirs = front_call(
        where, lhs, halo_own, halo_other, staged, weight, out_weight, filt, rates
    )
    beside = [
        query_call(where, lhs, halo_own, halo_other, query_weight, filt),
        *[local_call(source, ends, rates, gain, part) for part in range(PARTS)],
    ]

    into = 0.0
    for level, axis in enumerate(reversed(SEQ)):
        arrived = round_the_ring(total, axis)
        beside[level], *arrived = lax.optimization_barrier((beside[level], *arrived))
        total = total_weights[RING * level] * total
        for k, part in enumerate(arrived):
            part = part.astype(F32)
            into = into + into_weights[(RING - 1) * level + k] * part
            total = total + total_weights[RING * level + k + 1] * part

    hidden = hidden_call(into, beside[0], rates, beside[1:])
    return output_call(product_call(hidden, mine), swapped(hidden), swapped(theirs))


def solution(mesh):
    cube = Mesh(mesh.devices.reshape(RING, RING, RING, 2), (*SEQ, "ch"))
    return jax.shard_map(
        on_device,
        mesh=cube,
        in_specs=(
            P(SEQ, "ch"),
            P(None, None, "ch"),
            P(None, None, "ch"),
            P("ch", None),
            P("ch", None),
            P("ch", None),
        ),
        out_specs=P(SEQ, "ch"),
        check_vma=False,
    )
```

```python
import functools

import jax
import jax.numpy as jnp
from jax import lax
from jax.experimental import pallas as pl
from jax.experimental.pallas import tpu as pltpu
from jax.sharding import Mesh, PartitionSpec as P

SEGS = 8
HALO = 16
LANES = 128
HISTORY = 8
WIDTH = 256
SEQ = ("z", "y", "x")
RING = 4
PARTS = 2
F32 = jnp.float32
BF16 = jnp.bfloat16
MIB = 1024 * 1024


def spread(row):
    return jnp.broadcast_to(row, (SEGS, row.shape[-1]))


def filtered_step(taps, now, one, two):
    return taps[0] * now + taps[1] * one + taps[2] * two


def tree_sum(parts):
    parts = list(parts)
    while len(parts) > 1:
        parts = [a + b for a, b in zip(parts[::2], parts[1::2])]
    return parts[0]


def stage_kernel(
    where_ref,
    own_ref,
    other_ref,
    w_ref,
    filt_ref,
    rates_ref,
    lhs_out,
    w_out,
    filt_out,
    rates_out,
    into_out,
    total_out,
    sems,
):
    rows, half = own_ref.shape
    core = lax.rem(where_ref[0], 2)
    mine = pl.multiple_of(core * half, half)
    theirs = pl.multiple_of((1 - core) * half, half)
    pairs = [
        (rates_ref, rates_out),
        (own_ref, lhs_out.at[:, pl.ds(mine, half)]),
        (other_ref, lhs_out.at[:, pl.ds(theirs, half)]),
        (filt_ref, filt_out),
        (w_ref.at[pl.ds(1, w_out.shape[0])], w_out),
    ]
    copies = [pltpu.make_async_copy(src, dst, sems.at[i]) for i, (src, dst) in enumerate(pairs)]
    for copy in copies:
        copy.start()
    copies[0].wait()
    rates = rates_out[...]
    rest, span, after = where_ref[0] // 2, rows, 0

    def decay(tokens):
        return jnp.exp(-rates * jnp.asarray(tokens, F32))

    for level in range(len(SEQ)):
        here = lax.rem(rest, RING)
        rest = rest // RING
        total_out[RING * level] = decay(span * (RING - 1 - here))
        for k in range(1, RING):
            inside = (k <= here).astype(F32)
            into_out[(RING - 1) * level + k - 1] = inside * decay(span * (k - 1) + after)
            place = lax.rem(here - k + RING, RING)
            total_out[RING * level + k] = decay(span * (RING - 1 - place))
        after = after + span * here
        span = span * RING
    for copy in copies[1:]:
        copy.wait()


def stage_call(where, own, other, weight, filt, rates):
    rows, half = own.shape
    vmem = pl.BlockSpec(memory_space=pltpu.VMEM)
    anywhere = pl.BlockSpec(memory_space=pl.ANY)
    inputs = [pltpu.with_memory_space_constraint(x, pltpu.HBM) for x in (own, weight, filt, rates)]
    return pl.pallas_call(
        stage_kernel,
        in_specs=[pl.BlockSpec(memory_space=pltpu.SMEM)] + [anywhere] * 5,
        out_specs=[vmem] * 6,
        out_shape=[
            pltpu.VMEM((rows, 2 * half), BF16),
            pltpu.VMEM((weight.shape[0] - 1, *weight.shape[1:]), BF16),
            pltpu.VMEM(filt.shape, F32),
            pltpu.VMEM(rates.shape, F32),
            pltpu.VMEM((len(SEQ) * (RING - 1), *rates.shape), F32),
            pltpu.VMEM((len(SEQ) * RING, *rates.shape), F32),
        ],
        scratch_shapes=[pltpu.SemaphoreType.DMA((5,))],
        compiler_params=pltpu.CompilerParams(vmem_limit_bytes=4 * MIB),
        name="stage",
    )(where, inputs[0], other, *inputs[1:])


def hold_segments(held, part, first, per):
    steps = held.shape[1] // SEGS - HISTORY
    pitch = steps + HISTORY
    for l in range(WIDTH // LANES):
        lanes = slice(l * LANES, (l + 1) * LANES)
        for g in range(first, first + per):
            row = (g - first) * steps + (0 if first else HALO)
            held[l, g * pitch + HISTORY : (g + 1) * pitch] = part[row : row + steps, lanes]
            if g == 0:
                held[l, :HISTORY] = part[row - HISTORY : row, lanes]
            if g + 1 < SEGS:
                held[l, (g + 1) * pitch : (g + 1) * pitch + HISTORY] = part[
                    row + steps - HISTORY : row + steps, lanes
                ]


def join_halo(where_ref, halo_ref, own_ref, other_ref):
    half = own_ref.shape[1]
    core = lax.rem(where_ref[0], 2)
    halo_ref[:, pl.ds(pl.multiple_of(core * half, half), half)] = own_ref[...]
    halo_ref[:, pl.ds(pl.multiple_of((1 - core) * half, half), half)] = other_ref[...]


def segment_rows(lhs_ref, halo_ref, first, per):
    steps = lhs_ref.shape[0] // SEGS
    rows = lhs_ref[first * steps : (first + per) * steps]
    return rows if first else jnp.concatenate([halo_ref[...], rows], axis=0)


def front_kernel(
    where_ref,
    lhs_ref,
    halo_own_ref,
    halo_other_ref,
    w_ref,
    filt_ref,
    rates_ref,
    source_ref,
    ends_ref,
    total_ref,
    halo_ref,
    proj_a,
    proj_b,
):
    rows = lhs_ref.shape[0]
    steps = rows // SEGS
    pitch = steps + HISTORY
    modes = rates_ref.shape[0]
    streams = w_ref.shape[0]
    tiles = w_ref.shape[2] // WIDTH
    per = SEGS // 2
    proj = (proj_a, proj_b)

    join_halo(where_ref, halo_ref, halo_own_ref, halo_other_ref)

    def projection(tile):
        held = proj[tile % 2]

        def piece(j, first):
            part = jnp.dot(
                segment_rows(lhs_ref, halo_ref, first, per),
                w_ref[j, :, tile * WIDTH : (tile + 1) * WIDTH],
                preferred_element_type=F32,
            )
            hold_segments(held.at[j], part, first, per)

        return [
            lambda j=j, first=first: piece(j, first)
            for j in range(streams)
            for first in range(0, SEGS, per)
        ]

    def recurrence(tile, size=4):
        held = proj[tile % 2]
        pieces = []
        for l in range(WIDTH // LANES):
            lanes = slice(tile * WIDTH + l * LANES, tile * WIDTH + (l + 1) * LANES)
            kept = {}

            def at(j, t, l=l):
                return held[j, l, pl.ds(HISTORY + t, SEGS, stride=pitch), :]

            def begin(kept=kept, lanes=lanes, at=at):
                kept["taps"] = [
                    [spread(filt_ref[a, j + 1 : j + 2, lanes]) for a in range(3)]
                    for j in range(streams)
                ]
                kept["decay"] = [spread(jnp.exp(-rates_ref[n : n + 1, lanes])) for n in range(modes)]
                kept["one"] = [at(j, -1) for j in range(streams)]
                kept["two"] = [at(j, -2) for j in range(streams)]
                kept["state"] = [jnp.zeros((SEGS, LANES), F32)] * modes

            def advance(t0, kept=kept, lanes=lanes, at=at):
                for t in range(t0, t0 + size):
                    now = [at(j, t) for j in range(streams)]
                    k, v = [
                        filtered_step(*terms)
                        for terms in zip(kept["taps"], now, kept["one"], kept["two"])
                    ]
                    kept["one"], kept["two"] = now, kept["one"]
                    source = k * v
                    kept["state"] = [d * s + source for d, s in zip(kept["decay"], kept["state"])]
                    source_ref[t * SEGS : (t + 1) * SEGS, lanes] = source

            def finish(kept=kept, lanes=lanes):
                seg = lax.broadcasted_iota(jnp.int32, (SEGS, LANES), 0)
                later = (SEGS - 1 - seg).astype(F32) * float(steps)
                for n, state in enumerate(kept["state"]):
                    ends_ref[n * SEGS : (n + 1) * SEGS, lanes] = state
                    weight = jnp.exp(-spread(rates_ref[n : n + 1, lanes]) * later)
                    total_ref[n : n + 1, lanes] = jnp.sum(state * weight, axis=0, keepdims=True)

            pieces += [begin]
            pieces += [lambda t0=t0, advance=advance: advance(t0) for t0 in range(0, steps, size)]
            pieces += [finish]
        return pieces

    for work in projection(0):
        work()
    for tile in range(tiles):
        slow = projection(tile + 1) if tile + 1 < tiles else [lambda: None]
        fast = recurrence(tile)
        done = 0
        for i, work in enumerate(slow):
            work()
            upto = (i + 1) * len(fast) // len(slow)
            for step in fast[done:upto]:
                step()
            done = upto


def front_call(where, lhs, halo_own, halo_other, staged, filt, rates):
    rows, full = lhs.shape
    streams, _, channels = staged.shape
    modes = rates.shape[0]
    vmem = pl.BlockSpec(memory_space=pltpu.VMEM)
    held = pltpu.VMEM((streams, WIDTH // LANES, rows + SEGS * HISTORY, LANES), F32)
    return pl.pallas_call(
        front_kernel,
        in_specs=[pl.BlockSpec(memory_space=pltpu.SMEM)]
        + [vmem] * 6,
        out_specs=[vmem] * 3,
        out_shape=[
            pltpu.VMEM((rows, channels), F32),
            pltpu.VMEM((modes * SEGS, channels), F32),
            pltpu.VMEM((modes, channels), F32),
        ],
        scratch_shapes=[pltpu.VMEM((HALO, full), BF16), held, held],
        compiler_params=pltpu.CompilerParams(vmem_limit_bytes=10 * MIB),
        name="front",
    )(
        where,
        lhs,
        halo_own,
        halo_other,
        staged,
        filt,
        rates,
    )


def query_kernel(where_ref, lhs_ref, halo_own_ref, halo_other_ref, w_ref, filt_ref, query_ref, halo_ref, held):
    steps = lhs_ref.shape[0] // SEGS
    pitch = steps + HISTORY
    per = SEGS // 2
    join_halo(where_ref, halo_ref, halo_own_ref, halo_other_ref)
    for tile in range(w_ref.shape[1] // WIDTH):
        for first in range(0, SEGS, per):
            part = jnp.dot(
                segment_rows(lhs_ref, halo_ref, first, per),
                w_ref[:, tile * WIDTH : (tile + 1) * WIDTH],
                preferred_element_type=F32,
            )
            hold_segments(held.at[tile], part, first, per)
        for l in range(WIDTH // LANES):
            lanes = slice(tile * WIDTH + l * LANES, tile * WIDTH + (l + 1) * LANES)
            taps = [spread(filt_ref[a, 0:1, lanes]) for a in range(3)]

            def at(t, tile=tile, l=l):
                return held[tile, l, pl.ds(HISTORY + t, SEGS, stride=pitch), :]

            one, two = at(-1), at(-2)
            for t in range(steps):
                now = at(t)
                query_ref[t * SEGS : (t + 1) * SEGS, lanes] = filtered_step(taps, now, one, two)
                one, two = now, one


def query_call(where, lhs, halo_own, halo_other, weight, filt):
    rows, full = lhs.shape
    channels = weight.shape[1]
    vmem = pl.BlockSpec(memory_space=pltpu.VMEM)
    args = [
        pltpu.with_memory_space_constraint(x, pltpu.VMEM)
        for x in (lhs, halo_own, halo_other, weight, filt)
    ]
    return pl.pallas_call(
        query_kernel,
        in_specs=[pl.BlockSpec(memory_space=pltpu.SMEM)] + [vmem] * 5,
        out_specs=vmem,
        out_shape=pltpu.VMEM((rows, channels), F32),
        scratch_shapes=[
            pltpu.VMEM((HALO, full), BF16),
            pltpu.VMEM((channels // WIDTH, WIDTH // LANES, rows + SEGS * HISTORY, LANES), F32),
        ],
        compiler_params=pltpu.CompilerParams(vmem_limit_bytes=6 * MIB),
        cost_estimate=pl.CostEstimate(
            flops=2 * (rows + HALO) * full * channels, transcendentals=0, bytes_accessed=0
        ),
        name="query",
    )(where, *args)


def local_kernel(
    first,
    carried,
    source_ref,
    ends_ref,
    rates_ref,
    gain_ref,
    *refs,
):
    copies = []
    if carried:
        refs, (w_ref, staged_ref, sem) = refs[1:4], (refs[0], *refs[4:])
        copies.append(pltpu.make_async_copy(w_ref.at[0], staged_ref, sem))
    for copy in copies:
        copy.start()
    local_ref, base_ref, factor_ref = refs
    rows, channels = local_ref.shape
    steps = rows // SEGS
    modes = rates_ref.shape[0]
    seg = lax.broadcasted_iota(jnp.int32, (SEGS, LANES), 0)
    for i in range(channels // LANES):
        lanes = slice(first + i * LANES, first + (i + 1) * LANES)
        here = slice(i * LANES, (i + 1) * LANES)
        rates = [spread(rates_ref[n : n + 1, lanes]) for n in range(modes)]
        gains = [spread(gain_ref[n : n + 1, lanes]) for n in range(modes)]
        for n in range(modes):
            mode = slice(n * SEGS, (n + 1) * SEGS)
            state = jnp.where(seg >= 1, pltpu.roll(ends_ref[mode, lanes], 1, 0), 0.0)
            for hop in (1, 2, 4):
                earlier = pltpu.roll(state, hop, 0) * jnp.exp(-rates[n] * float(steps * hop))
                state = state + jnp.where(seg >= hop, earlier, 0.0)
            base_ref[mode, here] = gains[n] * state
            factor_ref[mode, here] = gains[n] * jnp.exp(-rates[n] * (seg * steps).astype(F32))
        decays = [jnp.exp(-rate) for rate in rates]
        states = [jnp.zeros((SEGS, LANES), F32)] * modes
        for t in range(steps):
            row = slice(t * SEGS, (t + 1) * SEGS)
            source = source_ref[row, lanes]
            states = [d * s + source for d, s in zip(decays, states)]
            local_ref[row, here] = tree_sum([g * s for g, s in zip(gains, states)])
    for copy in copies:
        copy.wait()


def local_call(source, ends, rates, gain, part, weight=None):
    rows, channels = source.shape
    wide = channels // PARTS
    vmem = pl.BlockSpec(memory_space=pltpu.VMEM)
    args = [pltpu.with_memory_space_constraint(x, pltpu.VMEM) for x in (source, ends, rates, gain)]
    carried = weight is not None
    extra = [pltpu.with_memory_space_constraint(weight, pltpu.HBM)] if carried else []
    return pl.pallas_call(
        functools.partial(local_kernel, part * wide, carried),
        in_specs=[vmem] * 4 + [pl.BlockSpec(memory_space=pl.ANY)] * len(extra),
        out_specs=[vmem] * (3 + len(extra)),
        out_shape=[
            pltpu.VMEM((rows, wide), F32),
            pltpu.VMEM((ends.shape[0], wide), F32),
            pltpu.VMEM((ends.shape[0], wide), F32),
            *[pltpu.VMEM(x.shape[1:], BF16) for x in extra],
        ],
        scratch_shapes=[pltpu.SemaphoreType.DMA] * len(extra),
        compiler_params=pltpu.CompilerParams(vmem_limit_bytes=4 * MIB),
        cost_estimate=pl.CostEstimate(
            flops=4 * rates.shape[0] * rows * wide, transcendentals=0, bytes_accessed=0
        ),
        name="local",
    )(*args, *extra)


def hidden_kernel(into_ref, query_ref, rates_ref, *refs):
    hidden_ref = refs[-1]
    rows, channels = query_ref.shape
    modes = rates_ref.shape[0]
    wide = channels // PARTS
    for i in range(channels // LANES):
        lanes = slice(i * LANES, (i + 1) * LANES)
        part = i * LANES // wide
        local_ref, base_ref, factor_ref = refs[3 * part : 3 * part + 3]
        here = slice(lanes.start - part * wide, lanes.stop - part * wide)
        decays, leads = [], []
        for n in range(modes):
            mode = slice(n * SEGS, (n + 1) * SEGS)
            decays.append(spread(jnp.exp(-rates_ref[n : n + 1, lanes])))
            incoming = spread(into_ref[n : n + 1, lanes])
            leads.append(base_ref[mode, here] + factor_ref[mode, here] * incoming)
        for t in range(0, rows, 2 * SEGS):
            halves = []
            for row in (slice(t, t + SEGS), slice(t + SEGS, t + 2 * SEGS)):
                leads = [d * s for d, s in zip(decays, leads)]
                halves.append(query_ref[row, lanes] * (local_ref[row, here] + tree_sum(leads)))
            hidden_ref[t : t + 2 * SEGS, lanes] = jnp.concatenate(halves, axis=0).astype(BF16)


def hidden_call(into, query, rates, parts):
    vmem = pl.BlockSpec(memory_space=pltpu.VMEM)
    args = [
        pltpu.with_memory_space_constraint(x, pltpu.VMEM)
        for x in (into, query, rates, *(ref for part in parts for ref in part))
    ]
    return pl.pallas_call(
        hidden_kernel,
        in_specs=[vmem] * len(args),
        out_specs=vmem,
        out_shape=pltpu.VMEM(query.shape, BF16),
        compiler_params=pltpu.CompilerParams(vmem_limit_bytes=4 * MIB),
        name="hidden",
    )(*args)


def product_kernel(where_ref, hidden_ref, w_ref, w_other_ref, part_ref, staged_ref, mine_ref, sems):
    columns = part_ref.shape[1]
    lanes = pl.ds(pl.multiple_of(lax.rem(where_ref[0], 2) * columns, columns), columns)
    mine = pltpu.make_async_copy(w_ref.at[:, lanes], mine_ref, sems.at[0])
    theirs = pltpu.make_async_copy(w_other_ref.at[:, lanes], staged_ref, sems.at[1])
    mine.start()
    theirs.start()
    mine.wait()
    part_ref[...] = jnp.dot(hidden_ref[...], mine_ref[...], preferred_element_type=F32)
    theirs.wait()


def product_call(where, hidden, weight, weight_other):
    rows, channels = hidden.shape
    columns = weight.shape[1] // 2
    vmem = pl.BlockSpec(memory_space=pltpu.VMEM)
    anywhere = pl.BlockSpec(memory_space=pl.ANY)
    return pl.pallas_call(
        product_kernel,
        in_specs=[pl.BlockSpec(memory_space=pltpu.SMEM), vmem, anywhere, anywhere],
        out_specs=[vmem] * 2,
        out_shape=[pltpu.VMEM((rows, columns), F32), pltpu.VMEM((channels, columns), BF16)],
        scratch_shapes=[pltpu.VMEM((channels, columns), BF16), pltpu.SemaphoreType.DMA((2,))],
        compiler_params=pltpu.CompilerParams(vmem_limit_bytes=8 * MIB),
        name="product",
    )(where, hidden, weight, weight_other)


def output_kernel(part_ref, other_ref, w_ref, out_ref, acc_ref, rows_ref, sems):
    rows, columns = part_ref.shape
    steps = rows // SEGS
    copies = []
    for tile in range(columns // WIDTH):
        lanes = slice(tile * WIDTH, (tile + 1) * WIDTH)
        part = part_ref[:, lanes] + jnp.dot(
            other_ref[...], w_ref[:, lanes], preferred_element_type=F32
        )
        for l in range(WIDTH // LANES):
            acc_ref[tile, l] = part[:, l * LANES : (l + 1) * LANES]
            for j in range(SEGS):
                rows_ref[
                    j * steps : (j + 1) * steps,
                    tile * WIDTH + l * LANES : tile * WIDTH + (l + 1) * LANES,
                ] = acc_ref[tile, l, pl.ds(j, steps, stride=SEGS), :]
        copies.append(pltpu.make_async_copy(rows_ref.at[:, lanes], out_ref.at[:, lanes], sems.at[tile]))
        copies[-1].start()
    for copy in copies:
        copy.wait()


def output_call(part, other, weight):
    rows, columns = part.shape
    vmem = pl.BlockSpec(memory_space=pltpu.VMEM)
    args = [pltpu.with_memory_space_constraint(x, pltpu.VMEM) for x in (part, other, weight)]
    return pl.pallas_call(
        output_kernel,
        in_specs=[vmem] * 3,
        out_specs=pl.BlockSpec(memory_space=pl.ANY),
        out_shape=jax.ShapeDtypeStruct((rows, columns), F32),
        scratch_shapes=[
            pltpu.VMEM((columns // WIDTH, WIDTH // LANES, rows, LANES), F32),
            pltpu.VMEM((rows, columns), F32),
            pltpu.SemaphoreType.DMA((columns // WIDTH,)),
        ],
        compiler_params=pltpu.CompilerParams(vmem_limit_bytes=8 * MIB),
        name="output",
    )(*args)


def swapped(x):
    return lax.ppermute(x, "ch", [(0, 1), (1, 0)])


def from_before(x):
    count = RING**3
    return lax.ppermute(x, SEQ, [(i, i + 1) for i in range(count - 1)])


def round_the_ring(state, axis):
    sent = state.astype(BF16)
    return [
        lax.ppermute(sent, axis, [(i, (i + k) % RING) for i in range(RING)])
        for k in range(1, RING)
    ]


def on_device(tokens, in_weight, short_filter, residues, rates, out_weight):
    rows = tokens.shape[0]
    where = lax.axis_index((*SEQ, "ch")).astype(jnp.int32).reshape(1)
    weight = in_weight.transpose(1, 0, 2)
    rates = rates.T
    gain = residues.T * jnp.sqrt(1.0 - jnp.exp(-2.0 * rates))

    halo_own = from_before(tokens[rows - HALO :])
    lhs, staged, filt, rates, into_weights, total_weights = stage_call(
        where, tokens, swapped(tokens), weight, short_filter, rates
    )
    halo_own, lhs, out_weight = lax.optimization_barrier((halo_own, lhs, out_weight))
    halo_other = swapped(halo_own)
    lhs, halo_other, out_weight = lax.optimization_barrier((lhs, halo_other, out_weight))
    out_weight_other = swapped(out_weight)
    source, ends, total = front_call(where, lhs, halo_own, halo_other, staged, filt, rates)
    *first, query_weight = local_call(source, ends, rates, gain, 0, weight)
    query = query_call(where, lhs, halo_own, halo_other, query_weight, filt)
    second = local_call(source, ends, rates, gain, 1)
    beside = [tuple(first), query, tuple(second)]

    into = 0.0
    for level, axis in enumerate(reversed(SEQ)):
        arrived = round_the_ring(total, axis)
        beside[level], *arrived = lax.optimization_barrier((beside[level], *arrived))
        total = total_weights[RING * level] * total
        for k, part in enumerate(arrived):
            part = part.astype(F32)
            into = into + into_weights[(RING - 1) * level + k] * part
            total = total + total_weights[RING * level + k + 1] * part

    hidden = hidden_call(into, beside[1], rates, (beside[0], beside[2]))
    part, partner_weight = product_call(where, hidden, out_weight, out_weight_other)
    return output_call(part, swapped(hidden), partner_weight)


def solution(mesh):
    cube = Mesh(mesh.devices.reshape(RING, RING, RING, 2), (*SEQ, "ch"))
    return jax.shard_map(
        on_device,
        mesh=cube,
        in_specs=(
            P(SEQ, "ch"),
            P(None, None, "ch"),
            P(None, None, "ch"),
            P("ch", None),
            P("ch", None),
            P("ch", None),
        ),
        out_specs=P(SEQ, "ch"),
        check_vma=False,
    )
```
